256 devices in a mesh: patch: 16 (over x, y), member: 16 (over z, core).
Axes of the slice: x: 4, y: 4, z: 8, core: 2. Of those that a mesh axis runs over, the one named last changes fastest.
Arguments:
- init_field: float32 [1024, 256, 256], P('member', 'patch'), may hold values from -6 to 6
- flow_fields: float32 [4, 256, 256], P(None, 'patch'), may hold values from -6 to 6, as said below
- emission: float32 [1024], P('member'), may hold values from 0.5 to 2
- observed_cell: int32 [256, 512], P(('patch', 'member')), may hold values from 0 to 767
- observed_count: int32 [256], P(('patch', 'member')), may hold values from 1 to 512, as said below
- observed_value: float32 [256, 512], P(('patch', 'member')), may hold values from -6 to 6
- observed_scale: float32 [256, 512], P(('patch', 'member')), may hold values from 0.1 to 10
Outputs:
- analysis: float32 [1024, 256, 256], P('member', 'patch')
The draws below stay inside these ranges and needn't reach their ends.
Inputs may be any that keep to these rules, and one draw needn't show every extreme that they name: `observed_cell`: A position is (row offset + 1) * 256 + column with row offset -1, 0 or 1 from the region's row; slots from observed_count on are not read. `observed_count`: some region has 512 observations and some region has one. `flow_fields`: rows 0 and 1 lie in -0.5 to 0.5, row 2 in 0.02 to 0.5.
All inputs are finite; a program needn't handle non-finite values.
Results may differ from the reference program's by a relative error of at most 0.0012.
Values sent between devices are 32-bit elements; how exact they have to be, the bound alone decides.
A program may use at most 64 MiB of HBM per device.

```python
import math
import jax
import jax.numpy as jnp
from jax import lax

ENSEMBLE = 1024
NY = 256
SLOTS = 512
STEPS = 2
NX = 256


def draw_flow_fields(key, part):
    keys = jax.random.split(jax.random.fold_in(key, 7), 4)
    shape = (NX, NY)
    row_flow = jax.random.uniform(keys[0], shape, jnp.float32, -0.5, 0.5)
    col_flow = jax.random.uniform(keys[1], shape, jnp.float32, -0.5, 0.5)
    decay_rate = jnp.exp(jax.random.uniform(keys[2], shape, jnp.float32, math.log(0.02), math.log(0.5)))
    source = jax.random.normal(keys[3], shape, jnp.float32)
    row_flow = jnp.clip(row_flow, -0.5, 0.5)
    col_flow = jnp.clip(col_flow, -0.5, 0.5)
    decay_rate = jnp.clip(decay_rate, 0.02, 0.5)
    source = jnp.clip(source, -6.0, 6.0)
    return jnp.stack([row_flow, col_flow, decay_rate, source]).astype(jnp.float32)


def draw_observed_count(key, part):
    first, second = jax.random.split(jax.random.fold_in(key, 11))
    counts = jax.random.randint(first, (NX,), 1, SLOTS + 1)
    order = jax.random.permutation(second, NX)
    counts = counts.at[order[0]].set(SLOTS)
    counts = counts.at[order[1]].set(1)
    return counts.astype(jnp.int32)


def with_ends(entries, rng, low, largest):
    longest = entries.shape.index(max(entries.shape))
    spots = []
    for shift in (0, 1):
        where = [jax.random.randint(jax.random.fold_in(rng, axis), (), 0, length) for axis, length in enumerate(entries.shape)]
        where[longest] = (where[longest] + shift) % entries.shape[longest]
        spots.append(tuple(where))
    return entries.at[spots[0]].set(low).at[spots[1]].set(largest)


def level_of(rng, extent, pieces, least, top_value):
    gain, own = 1.0, jax.random.fold_in(rng, 6)
    for dim, shards_of in pieces:
        heights = jnp.exp(jax.random.uniform(jax.random.fold_in(own, dim), (shards_of,), jnp.float32, least / len(pieces), top_value / len(pieces)))
        gain = gain * jnp.repeat(heights, extent[dim] // shards_of).reshape([-1 if axis == dim else 1 for axis in range(len(extent))])
    return gain


def noise(stream_key, dims, deviation, limit, shards=(), held_as=jnp.bfloat16):
    factor_of = level_of(stream_key, dims, shards, -0.22, 0.18) if shards else 1.0
    drawn = jax.random.normal(stream_key, dims, jnp.float32) * deviation * factor_of
    return jnp.minimum(jnp.maximum(drawn, -limit), limit).astype(held_as)


def setup_inputs(seed: int = 0) -> dict:
    key_of = jax.random.split(jax.random.key(seed), 8)
    return {
        "init_field": noise(key_of[0], (ENSEMBLE, NX, NY), 1.0, 6.0, ((0, 16), (1, 16)), jnp.float32),
        "flow_fields": draw_flow_fields(jax.random.fold_in(key_of[7], 71), 0),
        "emission": jnp.clip(jnp.exp(math.log(2.0) - 1.3862944 * jax.random.uniform(key_of[2], (ENSEMBLE,), jnp.float32) ** level_of(key_of[2], (ENSEMBLE,), ((0, 16),), -0.2, 0.2)), 0.5, 2.0),
        "observed_cell": with_ends(jax.random.randint(key_of[3], (NX, SLOTS), 0, 3 * NY), jax.random.fold_in(key_of[3], 1), 0, (3 * NY) - 1).astype(jnp.int32),
        "observed_count": draw_observed_count(jax.random.fold_in(key_of[7], 71), 0),
        "observed_value": noise(key_of[5], (NX, SLOTS), 1.0, 6.0, ((0, 256),), jnp.float32),
        "observed_scale": jnp.clip(jnp.exp(math.log(10.0) - 4.6051702 * jax.random.uniform(key_of[6], (NX, SLOTS), jnp.float32) ** level_of(key_of[6], (NX, SLOTS), ((0, 256),), -0.2, 0.2)), 0.1, 10.0),
    }


HIGH = lax.Precision.HIGHEST

def advance(extended, flow_piece, emission):
    field = extended[:, 1:-1, :]
    behind_rows = extended[:, :-2, :]
    ahead_rows = extended[:, 2:, :]
    behind_cols = jnp.roll(field, 1, axis=2)
    ahead_cols = jnp.roll(field, -1, axis=2)
    row_flow = flow_piece[0]
    col_flow = flow_piece[1]
    advected = field - jnp.maximum(row_flow, 0.0) * (field - behind_rows) - jnp.minimum(row_flow, 0.0) * (ahead_rows - field) - jnp.maximum(col_flow, 0.0) * (field - behind_cols) - jnp.minimum(col_flow, 0.0) * (ahead_cols - field)
    return (1.0 - flow_piece[2]) * advected + emission[:, None, None] * flow_piece[3]

def analyse(window, cells, count, values, scales):
    members = window.shape[0]
    width = window.shape[1] // 3
    root = math.sqrt(members - 1)
    predicted = jnp.take(window, cells, axis=1)
    active_slot = (jnp.arange(cells.shape[0], dtype=jnp.int32) < count).astype(jnp.float32)
    slot_weight = active_slot * scales
    predicted_mean = lax.optimization_barrier(jnp.mean(predicted, axis=0))
    spread = (predicted - predicted_mean) * (slot_weight / root)
    innovation = slot_weight * (values - predicted_mean)
    own_row = window[:, width:2 * width]
    mean_row = lax.optimization_barrier(jnp.mean(own_row, axis=0))
    anomaly = own_row - mean_row
    forcing = jnp.dot(spread, innovation, precision=HIGH) / root
    weight_matrix = jnp.eye(members, dtype=jnp.float32) + jnp.dot(spread, spread.T, precision=HIGH)
    factor = jnp.linalg.cholesky(weight_matrix)
    solved = jax.scipy.linalg.cho_solve((factor, True), anomaly)
    weights = jax.scipy.linalg.cho_solve((factor, True), forcing)
    offset_term = jnp.dot(weights, anomaly, precision=HIGH)
    return mean_row + 0.5 * anomaly + 0.5 * solved + offset_term

def reference(init_field, flow_fields, emission, observed_cell, observed_count, observed_value, observed_scale):
    field = init_field
    for step_index in range(STEPS):
        padded = jnp.pad(field, ((0, 0), (1, 1), (0, 0)))
        field = advance(padded, flow_fields, emission)
    bordered = jnp.pad(field, ((0, 0), (1, 1), (0, 0)))

    def region(inputs):
        index, cells, count, values, scales = inputs
        window = lax.dynamic_slice_in_dim(bordered, index, 3, 1)
        window = window.reshape(ENSEMBLE, 3 * NY)
        return analyse(window, cells, count, values, scales)
    result = lax.map(region, (jnp.arange(NX, dtype=jnp.int32), observed_cell, observed_count, observed_value, observed_scale))
    return jnp.transpose(result, (1, 0, 2))
```

```python
import math

import jax
import jax.numpy as jnp
from jax import lax
from jax.experimental import pallas as pl
from jax.experimental.pallas import tpu as pltpu
from jax.sharding import PartitionSpec as P

STEPS = 2
F32=jnp.float32; BF=jnp.bfloat16
HIGH=lax.Precision.HIGHEST
NT=(((1,),(1,)),((),())); TN=(((0,),(0,)),((),())); NN=(((1,),(0,)),((),()))
def bdot(a,b,dims): return lax.dot_general(a,b,dims,preferred_element_type=F32)
def split2(x):
    hi=x.astype(BF); lo=(x-hi.astype(F32)).astype(BF)
    return hi,lo

def leaf_inverse(rows):
    G=len(rows)
    full=(8,128)
    lane=lax.broadcasted_iota(jnp.int32,full,1)
    sub=lax.broadcasted_iota(jnp.int32,full,0)
    for t in range(G):
        cols=[[jnp.broadcast_to(rows[g][:,8*t+j:8*t+j+1],full) for j in range(8)] for g in range(G)]
        el={}
        for i in range(8):
            for j in range(i,8):
                el[i,j]=jnp.broadcast_to(cols[t][j][i:i+1,:],full)
        piv=[jnp.broadcast_to(rows[t][i:i+1,:],full) for i in range(8)]
        def get(i,j): return el[(i,j) if i<=j else (j,i)]
        done=[False]*8
        def val(i,j):
            v=get(i,j)
            return v
        for p in range(8):
            r=1.0/el[p,p]
            cp=[get(i,p) for i in range(8)]
            sc=[None if i==p else cp[i]*r for i in range(8)]
            for i in range(8):
                for j in range(i,8):
                    if i==p or j==p: continue
                    el[i,j]=el[i,j]-cp[i]*sc[j]
            for i in range(8):
                if i!=p:
                    el[(i,p) if i<=p else (p,i)]=sc[i]
            el[p,p]=-r
        inpanel=(lane>=8*t)&(lane<8*t+8)
        new=[]
        unit=[jnp.where(lane==8*t+i,1.0,0.0).astype(F32) for i in range(8)]
        src=[jnp.where(inpanel,unit[i],piv[i]) for i in range(8)]
        for i in range(8):
            acc=[get(i,j)*src[j] for j in range(8)]
            while len(acc)>1: acc=[acc[a]+acc[a+1] for a in range(0,len(acc),2)]
            new.append(acc[0])
        out=[]
        for g in range(G):
            if g==t:
                o=new[7]
                for i in range(6,-1,-1): o=jnp.where(sub==i,new[i],o)
                out.append(-o)
            else:
                base=jnp.where(inpanel,0.0,rows[g])
                acc=[cols[g][i]*new[i] for i in range(8)]
                while len(acc)>1: acc=[acc[a]+acc[a+1] for a in range(0,len(acc),2)]
                out.append(base+acc[0])
        rows=out
    return rows

def solve_kernel(prev_ref, own_ref, next_ref, cell_ref, count_ref, value_ref, scale_ref, out_ref,
                 ahi, alo, gt_ref, shi, slo, T, D):
    members=own_ref.shape[0]; W=own_ref.shape[1]; C=3*W; SL=cell_ref.shape[1]
    root=math.sqrt(members-1)
    j=lax.broadcasted_iota(jnp.int32,(1,SL),1)
    act=jnp.where(j<count_ref[0],1.0,0.0).astype(F32)
    w=act*scale_ref[...]; w2=w*w; w2v=w2*value_ref[...]
    def split3(x):
        a=x.astype(BF).astype(F32); x=x-a; b=x.astype(BF).astype(F32); return a,b,x-b
    a0,a1,a2=split3(w2); b0,b1,b2=split3(w2v)
    lhs=jnp.concatenate([a0,a1,a2,b0,b1,b2,act,jnp.zeros_like(act)],axis=0).astype(BF)
    et=(lax.broadcasted_iota(jnp.int32,(C,SL),0)==cell_ref[...]).astype(F32).astype(BF)
    sums=bdot(lhs,et,NT)
    lam=sums[0:1]+sums[1:2]+sums[2:3]
    bet=sums[3:4]+sums[4:5]+sums[5:6]
    present=sums[6:7]>0.5
    pres8=jnp.broadcast_to(jnp.where(present,1.0,0.0),(8,C)).astype(BF)
    tri=(lax.broadcasted_iota(jnp.int32,(C,C),0)<=lax.broadcasted_iota(jnp.int32,(C,C),1)).astype(F32).astype(BF)
    rank=bdot(pres8,tri,NN)[0:1]
    slot=jnp.where(present,rank-1.0,-1.0).astype(jnp.int32)
    gt_ref[...]=(lax.broadcasted_iota(jnp.int32,(SL,C),0)==slot).astype(F32).astype(BF)
    s=jnp.sqrt(lam)
    mus=[]
    for q,ref in enumerate((prev_ref,own_ref,next_ref)):
        x=ref[...]
        mu=jnp.sum(x,axis=0,keepdims=True)*(1.0/members)
        mus.append(mu)
        sl=slice(q*W,(q+1)*W)
        h,l=split2((x-mu)*(s[:,sl]*(1.0/root)))
        ahi[:,sl]=h; alo[:,sl]=l
    mu=jnp.concatenate(mus,axis=1)
    d=jnp.where(present,(bet-lam*mu)/jnp.where(present,s,1.0),0.0)*(1.0/root)
    gt=gt_ref[...]
    shi[...]=bdot(gt,ahi[...],NT).astype(BF)
    slo[...]=bdot(gt,alo[...],NT).astype(BF)
    h,l=shi[...],slo[...]
    eye=(lax.broadcasted_iota(jnp.int32,(SL,SL),0)==lax.broadcasted_iota(jnp.int32,(SL,SL),1)).astype(F32)
    T[:,0:SL]=eye+bdot(h,h,NT)+(bdot(h,l,NT)+bdot(l,h,NT))
    oh,ol=split2(own_ref[...]-mus[1])
    T[:,SL:]=bdot(h,oh,NN)+(bdot(h,ol,NN)+bdot(l,oh,NN))
    def step(k,_):
        o=pl.multiple_of(k*128,128)
        blk=T[pl.ds(o,128),pl.ds(o,128)]
        rows=leaf_inverse([blk[8*g:8*g+8] for g in range(16)])
        dinv=jnp.concatenate(rows,axis=0)
        U=jnp.dot(dinv,T[pl.ds(o,128),:],precision=HIGH,preferred_element_type=F32)
        Cc=T[:,pl.ds(o,128)]
        T[...]=T[...]-jnp.dot(Cc,U,precision=HIGH,preferred_element_type=F32)
        T[pl.ds(o,128),:]=U
        return 0
    lax.fori_loop(0,SL//128,step,0)
    yh,yl=split2(T[:,SL:])
    zh=bdot(gt,yh,TN); zl=bdot(gt,yl,TN)
    off=jnp.dot(jnp.broadcast_to(d,(8,C)),zh+zl,precision=HIGH,preferred_element_type=F32)[0:1]
    zh=zh.astype(BF); zl=zl.astype(BF)
    sy=bdot(ahi[...],zh,NN)+(bdot(ahi[...],zl,NN)+bdot(alo[...],zh,NN))
    out_ref[...]=own_ref[...]-0.5*sy+off

def solve(prev,own,nxt,cells,count,values,scales):
    m,W=own.shape; SL=cells.shape[1]; C=3*W
    V=pl.BlockSpec(memory_space=pltpu.VMEM)
    return pl.pallas_call(solve_kernel,out_shape=jax.ShapeDtypeStruct((m,W),F32),
        in_specs=[V,V,V,V,pl.BlockSpec(memory_space=pltpu.SMEM),V,V],out_specs=V,
        scratch_shapes=[pltpu.VMEM((m,C),BF),pltpu.VMEM((m,C),BF),pltpu.VMEM((SL,C),BF),pltpu.VMEM((SL,m),BF),pltpu.VMEM((SL,m),BF),
                        pltpu.VMEM((SL,SL+W),F32),pltpu.VMEM((128,128),F32)],
        compiler_params=pltpu.CompilerParams(vmem_limit_bytes=60<<20),name='solve')(prev,own,nxt,cells,count,values,scales)


def padded(cells, sides, width):
    for axis, dim in sides:
        count = lax.axis_size(axis)
        ends = count - 1
        head = lax.slice_in_dim(cells, 0, width, axis=dim)
        tail = lax.slice_in_dim(cells, cells.shape[dim] - width, cells.shape[dim], axis=dim)
        cells = jnp.concatenate(
            [
                lax.ppermute(tail, axis, [(i, (i + 1) % count) for i in range(ends)]),
                cells,
                lax.ppermute(head, axis, [((i + 1) % count, i) for i in range(ends)]),
            ],
            axis=dim,
        )
    return cells


def advance(extended, flow_piece, emission):
    field = extended[:, 1:-1, :]
    behind_rows = extended[:, :-2, :]
    ahead_rows = extended[:, 2:, :]
    behind_cols = jnp.roll(field, 1, axis=2)
    ahead_cols = jnp.roll(field, -1, axis=2)
    row_flow = flow_piece[0]
    col_flow = flow_piece[1]
    advected = (
        field
        - jnp.maximum(row_flow, 0.0) * (field - behind_rows)
        - jnp.minimum(row_flow, 0.0) * (ahead_rows - field)
        - jnp.maximum(col_flow, 0.0) * (field - behind_cols)
        - jnp.minimum(col_flow, 0.0) * (ahead_cols - field)
    )
    return (1.0 - flow_piece[2]) * advected + emission[:, None, None] * flow_piece[3]


def per_device(
    init_field, flow_fields, emission, observed_cell, observed_count, observed_value, observed_scale
):
    field = init_field
    for step_index in range(STEPS):
        extended = padded(field, (("patch", 1),), 1)
        field = advance(extended, flow_fields, emission)
    regrouped = lax.all_to_all(field, "member", split_axis=1, concat_axis=0, tiled=True)
    bordered = padded(regrouped, ((("patch", "member"), 1),), 1)
    rows = bordered
    analysed = solve(rows[:, 0], rows[:, 1], rows[:, 2], observed_cell, observed_count, observed_value, observed_scale)
    return lax.all_to_all(
        analysed[:, None, :], "member", split_axis=0, concat_axis=1, tiled=True
    )


def solution(mesh):
    return jax.shard_map(
        per_device,
        mesh=mesh,
        in_specs=(
            P("member", "patch", None),
            P(None, "patch", None),
            P("member"),
            P(("patch", "member"), None),
            P(("patch", "member")),
            P(("patch", "member"), None),
            P(("patch", "member"), None),
        ),
        out_specs=P("member", "patch", None),
        check_vma=False,
    )
```

```python
import functools
import math

import jax
import jax.numpy as jnp
from jax import lax
from jax.experimental import pallas as pl
from jax.experimental.pallas import tpu as pltpu
from jax.sharding import PartitionSpec as P

F32=jnp.float32; BF=jnp.bfloat16
HIGH=lax.Precision.HIGHEST
NT=(((1,),(1,)),((),())); TN=(((0,),(0,)),((),())); NN=(((1,),(0,)),((),()))
def bdot(a,b,dims): return lax.dot_general(a,b,dims,preferred_element_type=F32)
def split2(x):
    hi=x.astype(BF); lo=(x-hi.astype(F32)).astype(BF)
    return hi,lo

def leaf_inverse(rows):
    G=len(rows)
    full=(8,128)
    lane=lax.broadcasted_iota(jnp.int32,full,1)
    sub=lax.broadcasted_iota(jnp.int32,full,0)
    for t in range(G):
        cols=[[jnp.broadcast_to(rows[g][:,8*t+j:8*t+j+1],full) for j in range(8)] for g in range(G)]
        el={}
        for i in range(8):
            for j in range(i,8):
                el[i,j]=jnp.broadcast_to(cols[t][j][i:i+1,:],full)
        piv=[jnp.broadcast_to(rows[t][i:i+1,:],full) for i in range(8)]
        def get(i,j): return el[(i,j) if i<=j else (j,i)]
        done=[False]*8
        def val(i,j):
            v=get(i,j)
            return v
        for p in range(8):
            r=1.0/el[p,p]
            cp=[get(i,p) for i in range(8)]
            sc=[None if i==p else cp[i]*r for i in range(8)]
            for i in range(8):
                for j in range(i,8):
                    if i==p or j==p: continue
                    el[i,j]=el[i,j]-cp[i]*sc[j]
            for i in range(8):
                if i!=p:
                    el[(i,p) if i<=p else (p,i)]=sc[i]
            el[p,p]=-r
        inpanel=(lane>=8*t)&(lane<8*t+8)
        new=[]
        unit=[jnp.where(lane==8*t+i,1.0,0.0).astype(F32) for i in range(8)]
        src=[jnp.where(inpanel,unit[i],piv[i]) for i in range(8)]
        for i in range(8):
            acc=[get(i,j)*src[j] for j in range(8)]
            while len(acc)>1: acc=[acc[a]+acc[a+1] for a in range(0,len(acc),2)]
            new.append(acc[0])
        out=[]
        for g in range(G):
            if g==t:
                o=new[7]
                for i in range(6,-1,-1): o=jnp.where(sub==i,new[i],o)
                out.append(-o)
            else:
                base=jnp.where(inpanel,0.0,rows[g])
                acc=[cols[g][i]*new[i] for i in range(8)]
                while len(acc)>1: acc=[acc[a]+acc[a+1] for a in range(0,len(acc),2)]
                out.append(base+acc[0])
        rows=out
    return rows

def solve_kernel(even_ref, own_ref, outer_ref, inner_ref, cell_ref, count_ref, value_ref, scale_ref, out_ref,
                 ahi, alo, gt_ref, shi, slo, T, D):
    members=own_ref.shape[0]; W=own_ref.shape[1]; C=3*W; SL=cell_ref.shape[1]
    root=math.sqrt(members-1)
    j=lax.broadcasted_iota(jnp.int32,(1,SL),1)
    act=jnp.where(j<count_ref[0],1.0,0.0).astype(F32)
    w=act*scale_ref[...]; w2=w*w; w2v=w2*value_ref[...]
    def split3(x):
        a=x.astype(BF).astype(F32); x=x-a; b=x.astype(BF).astype(F32); return a,b,x-b
    a0,a1,a2=split3(w2); b0,b1,b2=split3(w2v)
    lhs=jnp.concatenate([a0,a1,a2,b0,b1,b2,act,jnp.zeros_like(act)],axis=0).astype(BF)
    cell=cell_ref[...]
    swapped=jnp.where(cell<W,cell+2*W,jnp.where(cell<2*W,cell,cell-2*W))
    cell=jnp.where(even_ref[0]==1,cell,swapped)
    et=(lax.broadcasted_iota(jnp.int32,(C,SL),0)==cell).astype(F32).astype(BF)
    sums=bdot(lhs,et,NT)
    lam=sums[0:1]+sums[1:2]+sums[2:3]
    bet=sums[3:4]+sums[4:5]+sums[5:6]
    present=sums[6:7]>0.5
    pres8=jnp.broadcast_to(jnp.where(present,1.0,0.0),(8,C)).astype(BF)
    tri=(lax.broadcasted_iota(jnp.int32,(C,C),0)<=lax.broadcasted_iota(jnp.int32,(C,C),1)).astype(F32).astype(BF)
    rank=bdot(pres8,tri,NN)[0:1]
    slot=jnp.where(present,rank-1.0,-1.0).astype(jnp.int32)
    gt_ref[...]=(lax.broadcasted_iota(jnp.int32,(SL,C),0)==slot).astype(F32).astype(BF)
    s=jnp.sqrt(lam)
    mus=[]
    for q,ref in enumerate((outer_ref,own_ref,inner_ref)):
        x=ref[...]
        mu=jnp.sum(x,axis=0,keepdims=True)*(1.0/members)
        mus.append(mu)
        sl=slice(q*W,(q+1)*W)
        h,l=split2((x-mu)*(s[:,sl]*(1.0/root)))
        ahi[:,sl]=h; alo[:,sl]=l
    mu=jnp.concatenate(mus,axis=1)
    d=jnp.where(present,(bet-lam*mu)/jnp.where(present,s,1.0),0.0)*(1.0/root)
    gt=gt_ref[...]
    shi[...]=bdot(gt,ahi[...],NT).astype(BF)
    slo[...]=bdot(gt,alo[...],NT).astype(BF)
    h,l=shi[...],slo[...]
    eye=(lax.broadcasted_iota(jnp.int32,(SL,SL),0)==lax.broadcasted_iota(jnp.int32,(SL,SL),1)).astype(F32)
    T[:,0:SL]=eye+bdot(h,h,NT)+(bdot(h,l,NT)+bdot(l,h,NT))
    oh,ol=split2(own_ref[...]-mus[1])
    T[:,SL:]=bdot(h,oh,NN)+(bdot(h,ol,NN)+bdot(l,oh,NN))
    def step(k,_):
        o=pl.multiple_of(k*128,128)
        blk=T[pl.ds(o,128),pl.ds(o,128)]
        rows=leaf_inverse([blk[8*g:8*g+8] for g in range(16)])
        dinv=jnp.concatenate(rows,axis=0)
        U=jnp.dot(dinv,T[pl.ds(o,128),:],precision=HIGH,preferred_element_type=F32)
        Cc=T[:,pl.ds(o,128)]
        T[...]=T[...]-jnp.dot(Cc,U,precision=HIGH,preferred_element_type=F32)
        T[pl.ds(o,128),:]=U
        return 0
    lax.fori_loop(0,SL//128,step,0)
    yh,yl=split2(T[:,SL:])
    zh=bdot(gt,yh,TN); zl=bdot(gt,yl,TN)
    off=jnp.dot(jnp.broadcast_to(d,(8,C)),zh+zl,precision=HIGH,preferred_element_type=F32)[0:1]
    zh=zh.astype(BF); zl=zl.astype(BF)
    sy=bdot(ahi[...],zh,NN)+(bdot(ahi[...],zl,NN)+bdot(alo[...],zh,NN))
    out_ref[...]=own_ref[...]-0.5*sy+off

def solve(even,own,outer,inner,cells,count,values,scales):
    m,W=own.shape; SL=cells.shape[1]; C=3*W
    V=pl.BlockSpec(memory_space=pltpu.VMEM); S=pl.BlockSpec(memory_space=pltpu.SMEM)
    return pl.pallas_call(solve_kernel,out_shape=jax.ShapeDtypeStruct((m,W),F32),
        in_specs=[S,V,V,V,V,S,V,V],out_specs=V,
        scratch_shapes=[pltpu.VMEM((m,C),BF),pltpu.VMEM((m,C),BF),pltpu.VMEM((SL,C),BF),pltpu.VMEM((SL,m),BF),pltpu.VMEM((SL,m),BF),
                        pltpu.VMEM((SL,SL+W),F32),pltpu.VMEM((128,128),F32)],
        compiler_params=pltpu.CompilerParams(vmem_limit_bytes=60<<20),name='solve')(even,own,outer,inner,cells,count,values,scales)


MESH=pl.DeviceIdType.MESH

def forecast_kernel(x_ref, fl_ref, em_ref, out_ref, xa, xb, fb, g1, flx, sbuf, rbuf, ssem, rsem, lsem):
    P_=lax.axis_size('patch'); p=lax.axis_index('patch'); m=lax.axis_index('member')
    Bn=em_ref.shape[1]; R=x_ref.shape[0]//Bn; W=x_ref.shape[1]
    loads=[pltpu.make_async_copy(x_ref.at[:,h*128:(h+1)*128],t,lsem.at[h]) for h,t in enumerate((xa,xb))]
    for c in loads: c.start()
    barrier=pltpu.get_barrier_semaphore()
    up,dn=lax.rem(p+1,P_),lax.rem(p+P_-1,P_)
    for q in (up,dn): pl.semaphore_signal(barrier,inc=1,device_id=(q,m),device_id_type=MESH)
    row=lambda r: jnp.concatenate([t[pl.ds(r,Bn,stride=R),:] for t in (xa,xb)],axis=1)
    for c in loads: c.wait()
    for i in range(3):
        sbuf[0,i*Bn:(i+1)*Bn]=row(i)
        sbuf[1,i*Bn:(i+1)*Bn]=row(R-3+i)
    for f in range(4):
        sbuf[0,3*Bn+2*f:3*Bn+2*f+2]=fl_ref[f,0:2]
        sbuf[1,3*Bn+2*f:3*Bn+2*f+2]=fl_ref[f,R-2:R]
    pl.semaphore_wait(barrier,2)
    cps=[]
    for k,q in ((0,dn),(1,up)):
        c=pltpu.make_async_remote_copy(src_ref=sbuf.at[k],dst_ref=rbuf.at[k],send_sem=ssem.at[k],recv_sem=rsem.at[k],device_id=(q,m),device_id_type=MESH)
        c.start(); cps.append(c)
    eye=lax.broadcasted_iota(jnp.int32,(Bn,Bn),0)==lax.broadcasted_iota(jnp.int32,(Bn,Bn),1)
    em=jnp.sum(jnp.where(eye,jnp.broadcast_to(em_ref[...],(Bn,Bn)),0.0),axis=1,keepdims=True)
    emb=jnp.broadcast_to(em,(Bn,W))
    for f in range(4): flx[f,2:2+R]=fl_ref[f]
    for r in range(R): fb[r+3]=row(r)
    mlo=jnp.where(p>0,1.0,0.0); mhi=jnp.where(p<P_-1,1.0,0.0)
    def step(f,b,a,i):
        rf=flx[0,pl.ds(i,1),:]; cf=flx[1,pl.ds(i,1),:]; dc=flx[2,pl.ds(i,1),:]; so=flx[3,pl.ds(i,1),:]
        bc=pltpu.roll(f,1,1); ac=pltpu.roll(f,W-1,1)
        adv=(f-jnp.maximum(rf,0.0)*(f-b)-jnp.minimum(rf,0.0)*(a-f)-jnp.maximum(cf,0.0)*(f-bc)-jnp.minimum(cf,0.0)*(ac-f))
        return (1.0-dc)*adv+emb*so
    def first(r,mask=None):
        v=step(fb[r+3],fb[r+2],fb[r+4],r+2)
        g1[r+2]=v if mask is None else v*mask
    def second(r,mask=None):
        v=step(g1[r+2],g1[r+1],g1[r+3],r+2)
        out_ref[r+1]=v if mask is None else v*mask
    lax.fori_loop(1,R-1,lambda r,_:(first(r),0)[1],0)
    lax.fori_loop(2,R-2,lambda r,_:(second(r),0)[1],0)
    for c in cps: c.wait()
    for i in range(3):
        fb[i]=rbuf[1,i*Bn:(i+1)*Bn]*mlo
        fb[R+3+i]=rbuf[0,i*Bn:(i+1)*Bn]*mhi
    for f in range(4):
        flx[f,0:2]=rbuf[1,3*Bn+2*f:3*Bn+2*f+2]
        flx[f,R+2:R+4]=rbuf[0,3*Bn+2*f:3*Bn+2*f+2]
    for r,k in ((-2,mlo),(-1,mlo),(0,None),(R-1,None),(R,mhi),(R+1,mhi)): first(r,k)
    for r,k in ((-1,mlo),(0,None),(1,None),(R-2,None),(R-1,None),(R,mhi)): second(r,k)

def forecast(x,fl,em):
    Bn,R,W=x.shape; V=pl.BlockSpec(memory_space=pltpu.VMEM)
    H=3*Bn+8
    return pl.pallas_call(forecast_kernel,out_shape=jax.ShapeDtypeStruct((R+2,Bn,W),F32),in_specs=[pl.BlockSpec(memory_space=pl.ANY),V,V],out_specs=V,
        scratch_shapes=[pltpu.VMEM((Bn*R,128),F32),pltpu.VMEM((Bn*R,128),F32),pltpu.VMEM((R+6,Bn,W),F32),pltpu.VMEM((R+4,Bn,W),F32),pltpu.VMEM((4,R+8,W),F32),pltpu.VMEM((2,H,W),F32),pltpu.VMEM((2,H,W),F32),
                        pltpu.SemaphoreType.DMA((2,)),pltpu.SemaphoreType.DMA((2,)),pltpu.SemaphoreType.DMA((2,))],
        compiler_params=pltpu.CompilerParams(collective_id=0,has_side_effects=True,vmem_limit_bytes=40<<20),name='forecast')(x.reshape(Bn*R,W),fl,em.reshape(1,Bn))

def gather_kernel(fc, own, outer, inner, ssend, sfwd, sin, rown, router, rinner):
    n=16
    p=lax.axis_index('patch'); m=lax.axis_index('member')
    B=fc.shape[1]; c=m//2; b=lax.rem(m,2); Z=n//2
    barrier=pltpu.get_barrier_semaphore()
    for d in range(1,n):
        pl.semaphore_signal(barrier,inc=1,device_id=(p,lax.rem(m+d,n)),device_id_type=MESH)
    pl.semaphore_wait(barrier,n-1)
    blk=lambda ref,s: ref.at[pl.ds(pl.multiple_of(s*B,B),B)]
    def push(src,dst,ss,rs,to):
        @pl.when(to==m)
        def _(): pltpu.make_async_copy(src,dst,rs).start()
        @pl.when(to!=m)
        def _(): pltpu.make_async_remote_copy(src_ref=src,dst_ref=dst,send_sem=ss,recv_sem=rs,device_id=(p,to),device_id_type=MESH).start()
    def sent(src,dst,ss,rs,to):
        @pl.when(to!=m)
        def _(): pltpu.make_async_remote_copy(src_ref=src,dst_ref=dst,send_sem=ss,recv_sem=rs,device_id=(p,to),device_id_type=MESH).wait_send()
    def landed(ref,s,rs):
        d=blk(ref,s); pltpu.make_async_copy(d,d,rs).wait()
    def even_row(cr):
        dl=lax.rem(c-cr+Z,Z); left=(dl>=Z//2)&(cr>0)
        return left, jnp.where(left,2*cr-1,2*cr)
    def odd_row(cr):
        dl=lax.rem(c-cr+Z,Z); right=(dl>=1)&(dl<=Z//2)&(cr<Z-1)
        return right, jnp.where(right,2*cr+2,2*cr+1)
    def sends(act):
        for k in range(Z):
            off=[4,3,5,2,6,1,7,0][k]
            cr=lax.rem(c+off,Z)
            for odd in (0,1):
                via,to=(odd_row if odd else even_row)(cr)
                r=2*cr+odd
                src=fc.at[r+1]; ss=ssend.at[r]
                @pl.when(via)
                def _(): act(src,blk(outer,m),ss,router.at[m],to)
                @pl.when(jnp.logical_not(via))
                def _(): act(src,blk(own,m),ss,rown.at[m],to)
        act(fc.at[0],blk(outer,m),ssend.at[n],router.at[m],0)
        act(fc.at[n+1],blk(outer,m),ssend.at[n+1],router.at[m],n-1)
    sends(push)
    edge=((b==0)&(c==0))|((b==1)&(c==Z-1))
    other=jnp.where(b==0,m+1,m-1)
    side=jnp.where(b==0,m-1,m+1)
    def relation(cs):
        dl=lax.rem(cs-c+Z,Z)
        own_far=jnp.where(b==0,dl>=Z//2,(dl>=1)&(dl<=Z//2))
        cn=jnp.where(b==0,c-1,c+1)
        do=lax.rem(cs-cn+2*Z,Z)
        out_near=jnp.where(b==0,(do>=1)&(do<=Z//2),do>=Z//2)
        return jnp.logical_not(own_far), out_near
    seq=[0,1,7,2,6,3,5,4]
    def forwards(act,wait):
        for off in seq:
            cs=lax.rem(c+off,Z)
            near,onear=relation(cs)
            for e in (0,1):
                s=2*cs+e
                @pl.when(onear&jnp.logical_not(edge))
                def _():
                    if wait: landed(outer,s,router.at[s])
                    act(blk(outer,s),blk(own,s),sfwd.at[s],rown.at[s],side)
                @pl.when(near)
                def _():
                    if wait: landed(own,s,rown.at[s])
                    act(blk(own,s),blk(inner,s),sin.at[s],rinner.at[s],other)
                    @pl.when(jnp.logical_not(edge))
                    def _(): act(blk(own,s),blk(outer,s),sfwd.at[n+s],router.at[s],side)
        for off in seq:
            cs=lax.rem(c+off,Z)
            near,onear=relation(cs)
            for e in (0,1):
                s=2*cs+e
                @pl.when(jnp.logical_not(near))
                def _():
                    if wait: landed(own,s,rown.at[s])
                    act(blk(own,s),blk(inner,s),sin.at[s],rinner.at[s],other)
    forwards(push,True)
    for off in seq:
        cs=lax.rem(c+off,Z)
        near,onear=relation(cs)
        for e in (0,1):
            s=2*cs+e
            @pl.when(jnp.logical_not(onear)|edge)
            def _(): landed(outer,s,router.at[s])
            landed(inner,s,rinner.at[s])
    sends(sent)
    forwards(sent,False)

def gather(fc):
    R2,B,W=fc.shape; n=R2-2; A=pl.BlockSpec(memory_space=pl.ANY); D=pltpu.SemaphoreType.DMA
    o=jax.ShapeDtypeStruct((n*B,W),F32)
    return pl.pallas_call(gather_kernel,out_shape=(o,o,o),in_specs=[A],out_specs=(A,A,A),
        scratch_shapes=[D((n+2,)),D((2*n,)),D((n,)),D((n,)),D((n,)),D((n,))],
        compiler_params=pltpu.CompilerParams(collective_id=1,has_side_effects=True),name='gather')(fc)

def scatter_kernel(x_ref, out_ref, ssem, rsem, lsem):
    p=lax.axis_index('patch'); m=lax.axis_index('member'); n=out_ref.shape[0]; B=out_ref.shape[1]
    barrier=pltpu.get_barrier_semaphore()
    for d in range(1,n):
        pl.semaphore_signal(barrier,inc=1,device_id=(p,lax.rem(m+d,n)),device_id_type=MESH)
    own=pltpu.make_async_copy(x_ref.at[pl.ds(pl.multiple_of(m*B,B),B)],out_ref.at[m],lsem)
    own.start()
    pl.semaphore_wait(barrier,n-1)
    cps=[]
    for d in [8,7,9,6,10,5,11,4,12,3,13,2,14,1,15]:
        to=lax.rem(m+d,n)
        c=pltpu.make_async_remote_copy(src_ref=x_ref.at[pl.ds(pl.multiple_of(to*B,B),B)],dst_ref=out_ref.at[m],
            send_sem=ssem.at[d],recv_sem=rsem.at[d],device_id=(p,to),device_id_type=MESH)
        c.start(); cps.append(c)
    own.wait()
    for c in cps: c.wait()
def scatter(x,n=16):
    A=pl.BlockSpec(memory_space=pl.ANY)
    return pl.pallas_call(scatter_kernel,out_shape=jax.ShapeDtypeStruct((n,x.shape[0]//n,x.shape[1]),F32),
      in_specs=[A],out_specs=A,scratch_shapes=[pltpu.SemaphoreType.DMA((n,)),pltpu.SemaphoreType.DMA((n,)),pltpu.SemaphoreType.DMA],
      compiler_params=pltpu.CompilerParams(collective_id=2,has_side_effects=True),name='scatter')(x)


def per_device(
    init_field, flow_fields, emission, observed_cell, observed_count, observed_value, observed_scale
):
    rows = forecast(init_field, flow_fields, emission)
    own, outer, inner = gather(rows)
    even = (lax.axis_index("member") % 2 == 0).astype(jnp.int32).reshape(1)
    analysed = solve(even, own, outer, inner, observed_cell, observed_count, observed_value, observed_scale)
    return jnp.transpose(scatter(analysed), (1, 0, 2))


def solution(mesh):
    return jax.shard_map(
        per_device,
        mesh=mesh,
        in_specs=(
            P("member", "patch", None),
            P(None, "patch", None),
            P("member"),
            P(("patch", "member"), None),
            P(("patch", "member")),
            P(("patch", "member"), None),
            P(("patch", "member"), None),
        ),
        out_specs=P("member", "patch", None),
        check_vma=False,
    )
```

```python
import functools
import math

import jax
import jax.numpy as jnp
from jax import lax
from jax.experimental import pallas as pl
from jax.experimental.pallas import tpu as pltpu
from jax.sharding import PartitionSpec as P

F32=jnp.float32; BF=jnp.bfloat16
HIGH=lax.Precision.HIGHEST
NT=(((1,),(1,)),((),())); TN=(((0,),(0,)),((),())); NN=(((1,),(0,)),((),()))
def bdot(a,b,dims): return lax.dot_general(a,b,dims,preferred_element_type=F32)
def split2(x):
    hi=x.astype(BF); lo=(x-hi.astype(F32)).astype(BF)
    return hi,lo

def tree(terms):
    while len(terms)>1:
        terms=[terms[a]+terms[a+1] if a+1<len(terms) else terms[a] for a in range(0,len(terms),2)]
    return terms[0]

def leaf_inverse(rows):
    G=len(rows); full=(8,128)
    lane=lax.broadcasted_iota(jnp.int32,full,1)
    sub=lax.broadcasted_iota(jnp.int32,full,0)
    down=lambda x,i: jnp.broadcast_to(x[i:i+1,:],full)
    for t in range(G):
        across=lambda g,j: jnp.broadcast_to(rows[g][:,8*t+j:8*t+j+1],full)
        inside=(lane>=8*t)&(lane<8*t+8)
        c=[across(t,j) for j in range(8)]
        src=[jnp.where(inside,jnp.where(lane==8*t+i,1.0,0.0),down(rows[t],i)) for i in range(8)]
        for p in range(8):
            r=1.0/down(c[p],p)
            at=sub==p
            mult=c[p]
            for j in range(8):
                if j==p: continue
                x=down(c[j],p)*r
                c[j]=jnp.where(at,x,c[j]-mult*x)
            c[p]=jnp.where(at,r,-(mult*r))
        new=tree([c[j]*src[j] for j in range(8)])
        rep=[down(new,i) for i in range(8)]
        out=[]
        for g in range(G):
            if g==t:
                out.append(new)
            else:
                out.append(jnp.where(inside,0.0,rows[g])-tree([across(g,i)*rep[i] for i in range(8)]))
        rows=out
    return rows

def solve_kernel(flag_ref, own_ref, outer_ref, inner_ref, obs_ref, out_ref,
                 ahi, alo, gt_ref, shi, slo, T):
    members=own_ref.shape[0]; W=own_ref.shape[1]; C=3*W; SL=obs_ref.shape[1]
    root=math.sqrt(members-1)
    j=lax.broadcasted_iota(jnp.int32,(1,SL),1)
    obs=obs_ref[...]
    act=jnp.where(j.astype(F32)<obs[1:2],1.0,0.0).astype(F32)
    w=act*obs[3:4]; w2=w*w; w2v=w2*obs[2:3]
    def split3(x):
        a=x.astype(BF).astype(F32); x=x-a; b=x.astype(BF).astype(F32); return a,b,x-b
    a0,a1,a2=split3(w2); b0,b1,b2=split3(w2v)
    lhs=jnp.concatenate([a0,a1,a2,b0,b1,b2,act,jnp.zeros_like(act)],axis=0).astype(BF)
    cell=obs[0:1].astype(jnp.int32)
    swapped=jnp.where(cell<W,cell+2*W,jnp.where(cell<2*W,cell,cell-2*W))
    cell=jnp.where(flag_ref[0]==1,cell,swapped)
    et=(lax.broadcasted_iota(jnp.int32,(C,SL),0)==cell).astype(F32).astype(BF)
    sums=bdot(lhs,et,NT)
    lam=sums[0:1]+sums[1:2]+sums[2:3]
    bet=sums[3:4]+sums[4:5]+sums[5:6]
    present=sums[6:7]>0.5
    pres8=jnp.broadcast_to(jnp.where(present,1.0,0.0),(8,C)).astype(BF)
    tri=(lax.broadcasted_iota(jnp.int32,(C,C),0)<=lax.broadcasted_iota(jnp.int32,(C,C),1)).astype(F32).astype(BF)
    rank=bdot(pres8,tri,NN)[0:1]
    slot=jnp.where(present,rank-1.0,-1.0).astype(jnp.int32)
    gt_ref[...]=(lax.broadcasted_iota(jnp.int32,(SL,C),0)==slot).astype(F32).astype(BF)
    s=jnp.sqrt(lam)
    mus=[]
    for q,ref in enumerate((outer_ref,own_ref,inner_ref)):
        x=ref[...]
        if q==0: x=jnp.where(flag_ref[1]==1,x,0.0)
        mu=jnp.sum(x,axis=0,keepdims=True)*(1.0/members)
        mus.append(mu)
        sl=slice(q*W,(q+1)*W)
        h,l=split2((x-mu)*(s[:,sl]*(1.0/root)))
        ahi[:,sl]=h; alo[:,sl]=l
    mu=jnp.concatenate(mus,axis=1)
    d=jnp.where(present,(bet-lam*mu)/jnp.where(present,s,1.0),0.0)*(1.0/root)
    gt=gt_ref[...]
    shi[...]=bdot(gt,ahi[...],NT).astype(BF)
    slo[...]=bdot(gt,alo[...],NT).astype(BF)
    h,l=shi[...],slo[...]
    eye=(lax.broadcasted_iota(jnp.int32,(SL,SL),0)==lax.broadcasted_iota(jnp.int32,(SL,SL),1)).astype(F32)
    T[:,0:SL]=eye+bdot(h,h,NT)+(bdot(h,l,NT)+bdot(l,h,NT))
    oh,ol=split2(own_ref[...]-mus[1])
    T[:,SL:]=bdot(h,oh,NN)+(bdot(h,ol,NN)+bdot(l,oh,NN))
    total=jnp.max(rank)
    def step(k):
        o=k*128
        rows=leaf_inverse([T[o+8*g:o+8*g+8,o:o+128] for g in range(16)])
        dinv=jnp.concatenate(rows,axis=0)
        cuts=[(o+128,o+256),(o+256,SL+W)] if o+128<SL else [(SL,SL+W)]
        for lo,hi in cuts:
            U=jnp.dot(dinv,T[o:o+128,lo:hi],precision=HIGH,preferred_element_type=F32)
            T[o:o+128,lo:hi]=U
            order=[i for i in range(SL//128) if i!=k]
            order=[i for i in order if i>k]+[i for i in order if i<k]
            for i in order:
                T[i*128:i*128+128,lo:hi]=T[i*128:i*128+128,lo:hi]-jnp.dot(T[i*128:i*128+128,o:o+128],U,precision=HIGH,preferred_element_type=F32)
    for k in range(3): step(k)
    @pl.when(total>384.5)
    def _(): step(3)
    yh,yl=split2(T[:,SL:])
    zh=bdot(gt,yh,TN); zl=bdot(gt,yl,TN)
    off=jnp.dot(jnp.broadcast_to(d,(8,C)),zh+zl,precision=HIGH,preferred_element_type=F32)[0:1]
    zh=zh.astype(BF); zl=zl.astype(BF)
    sy=bdot(ahi[...],zh,NN)+(bdot(ahi[...],zl,NN)+bdot(alo[...],zh,NN))
    out_ref[...]=own_ref[...]-0.5*sy+off

def solve(flags,own,outer,inner,obs):
    m,W=own.shape; SL=obs.shape[1]; C=3*W
    V=pl.BlockSpec(memory_space=pltpu.VMEM); S=pl.BlockSpec(memory_space=pltpu.SMEM)
    return pl.pallas_call(solve_kernel,out_shape=jax.ShapeDtypeStruct((m,W),F32),in_specs=[S,V,V,V,V],out_specs=V,
        scratch_shapes=[pltpu.VMEM((m,C),BF),pltpu.VMEM((m,C),BF),pltpu.VMEM((SL,C),BF),pltpu.VMEM((SL,m),BF),pltpu.VMEM((SL,m),BF),
                        pltpu.VMEM((SL,SL+W),F32)],
        compiler_params=pltpu.CompilerParams(vmem_limit_bytes=60<<20),name='solve')(flags,own,outer,inner,obs)


MESH=pl.DeviceIdType.MESH

def forecast_kernel(x_ref, fl_ref, em_ref, out_ref, xa, xb, fb, g1, flx, sbuf, rbuf, ssem, rsem, lsem):
    P_=lax.axis_size('patch'); p=lax.axis_index('patch'); m=lax.axis_index('member')
    Bn=em_ref.shape[1]; R=x_ref.shape[0]//Bn; W=x_ref.shape[1]
    loads=[pltpu.make_async_copy(x_ref.at[:,h*128:(h+1)*128],t,lsem.at[h]) for h,t in enumerate((xa,xb))]
    for c in loads: c.start()
    barrier=pltpu.get_barrier_semaphore()
    up,dn=lax.rem(p+1,P_),lax.rem(p+P_-1,P_)
    for q in (up,dn): pl.semaphore_signal(barrier,inc=1,device_id=(q,m),device_id_type=MESH)
    row=lambda r: jnp.concatenate([t[pl.ds(r,Bn,stride=R),:] for t in (xa,xb)],axis=1)
    for c in loads: c.wait()
    for i in range(2):
        sbuf[0,i*Bn:(i+1)*Bn]=row(i)
        sbuf[1,i*Bn:(i+1)*Bn]=row(R-2+i)
    for f in range(4):
        sbuf[0,2*Bn+2*f:2*Bn+2*f+2]=fl_ref[f,0:2]
        sbuf[1,2*Bn+2*f:2*Bn+2*f+2]=fl_ref[f,R-2:R]
    pl.semaphore_wait(barrier,2)
    cps=[]
    for k,q in ((0,dn),(1,up)):
        c=pltpu.make_async_remote_copy(src_ref=sbuf.at[k],dst_ref=rbuf.at[k],send_sem=ssem.at[k],recv_sem=rsem.at[k],device_id=(q,m),device_id_type=MESH)
        c.start(); cps.append(c)
    eye=lax.broadcasted_iota(jnp.int32,(Bn,Bn),0)==lax.broadcasted_iota(jnp.int32,(Bn,Bn),1)
    em=jnp.sum(jnp.where(eye,jnp.broadcast_to(em_ref[...],(Bn,Bn)),0.0),axis=1,keepdims=True)
    emb=jnp.broadcast_to(em,(Bn,W))
    for f in range(4): flx[f,2:2+R]=fl_ref[f]
    for r in range(R): fb[r+2]=row(r)
    mlo=jnp.where(p>0,1.0,0.0); mhi=jnp.where(p<P_-1,1.0,0.0)
    def step(f,b,a,i):
        rf=flx[0,pl.ds(i,1),:]; cf=flx[1,pl.ds(i,1),:]; dc=flx[2,pl.ds(i,1),:]; so=flx[3,pl.ds(i,1),:]
        bc=pltpu.roll(f,1,1); ac=pltpu.roll(f,W-1,1)
        adv=(f-jnp.maximum(rf,0.0)*(f-b)-jnp.minimum(rf,0.0)*(a-f)-jnp.maximum(cf,0.0)*(f-bc)-jnp.minimum(cf,0.0)*(ac-f))
        return (1.0-dc)*adv+emb*so
    def first(r,mask=None):
        v=step(fb[r+2],fb[r+1],fb[r+3],r+2)
        g1[r+1]=v if mask is None else v*mask
    def second(r):
        out_ref[r]=step(g1[r+1],g1[r],g1[r+2],r+2)
    lax.fori_loop(1,R-1,lambda r,_:(first(r),0)[1],0)
    lax.fori_loop(2,R-2,lambda r,_:(second(r),0)[1],0)
    for c in cps: c.wait()
    for i in range(2):
        fb[i]=rbuf[1,i*Bn:(i+1)*Bn]*mlo
        fb[R+2+i]=rbuf[0,i*Bn:(i+1)*Bn]*mhi
    for f in range(4):
        flx[f,0:2]=rbuf[1,2*Bn+2*f:2*Bn+2*f+2]
        flx[f,R+2:R+4]=rbuf[0,2*Bn+2*f:2*Bn+2*f+2]
    for r,k in ((-1,mlo),(0,None),(R-1,None),(R,mhi)): first(r,k)
    for r in (0,1,R-2,R-1): second(r)

def forecast(x,fl,em):
    Bn,R,W=x.shape; V=pl.BlockSpec(memory_space=pltpu.VMEM)
    H=2*Bn+8
    return pl.pallas_call(forecast_kernel,out_shape=jax.ShapeDtypeStruct((R,Bn,W),F32),in_specs=[pl.BlockSpec(memory_space=pl.ANY),V,V],out_specs=V,
        scratch_shapes=[pltpu.VMEM((Bn*R,128),F32),pltpu.VMEM((Bn*R,128),F32),pltpu.VMEM((R+4,Bn,W),F32),pltpu.VMEM((R+2,Bn,W),F32),pltpu.VMEM((4,R+8,W),F32),pltpu.VMEM((2,H,W),F32),pltpu.VMEM((2,H,W),F32),
                        pltpu.SemaphoreType.DMA((2,)),pltpu.SemaphoreType.DMA((2,)),pltpu.SemaphoreType.DMA((2,))],
        compiler_params=pltpu.CompilerParams(collective_id=0,has_side_effects=True,vmem_limit_bytes=40<<20),name='forecast')(x.reshape(Bn*R,W),fl,em.reshape(1,Bn))

def place(p,l):
    return jnp.where(lax.rem(p,2)==0,l,15-l)

def gather_kernel(fc, obs, own, outer, inner, obs_out, ssend, sfwd, sin, rown, router, rinner, sobs, robs):
    n=16
    P_=lax.axis_size('patch'); p=lax.axis_index('patch'); m=lax.axis_index('member')
    B=fc.shape[1]; Z=n//2
    l=place(p,m); c=l//2; b=lax.rem(l,2)
    first=(b==0)&(c==0); last=(b==1)&(c==Z-1); edge=first|last
    open_=jnp.logical_not((first&(p==0))|(last&(p==P_-1)))
    next_patch=jnp.where(first,p-1,p+1)
    barrier=pltpu.get_barrier_semaphore()
    for d in range(1,n):
        pl.semaphore_signal(barrier,inc=1,device_id=(p,lax.rem(m+d,n)),device_id_type=MESH)
    @pl.when(edge&open_)
    def _():
        pl.semaphore_signal(barrier,inc=1,device_id=(next_patch,m),device_id_type=MESH)
        pl.semaphore_wait(barrier,n)
    @pl.when(jnp.logical_not(edge&open_))
    def _(): pl.semaphore_wait(barrier,n-1)
    blk=lambda ref,s: ref.at[pl.ds(pl.multiple_of(s*B,B),B)]
    def remote(src,dst,ss,rs,to,tp=None):
        return pltpu.make_async_remote_copy(src_ref=src,dst_ref=dst,send_sem=ss,recv_sem=rs,device_id=(p if tp is None else tp,to),device_id_type=MESH)
    def push(src,dst,ss,rs,to):
        @pl.when(to==m)
        def _(): pltpu.make_async_copy(src,dst,rs).start()
        @pl.when(to!=m)
        def _(): remote(src,dst,ss,rs,to).start()
    def sent(src,dst,ss,rs,to):
        @pl.when(to!=m)
        def _(): remote(src,dst,ss,rs,to).wait_send()
    def landed(ref,s,rs):
        d=blk(ref,s); pltpu.make_async_copy(d,d,rs).wait()
    def even_row(cr):
        dl=lax.rem(c-cr+Z,Z); left=(dl>=Z//2)&(cr>0)
        return left, place(p,jnp.where(left,2*cr-1,2*cr))
    def odd_row(cr):
        dl=lax.rem(c-cr+Z,Z); right=(dl>=1)&(dl<=Z//2)&(cr<Z-1)
        return right, place(p,jnp.where(right,2*cr+2,2*cr+1))
    NEAR=[0,1,7,2,6,3,5,4]
    def sends(act):
        for off in NEAR:
            cr=lax.rem(c+off,Z)
            for odd in (0,1):
                via,to=(odd_row if odd else even_row)(cr)
                r=2*cr+odd
                src=fc.at[r]; ss=ssend.at[r]
                @pl.when(via)
                def _(): act(src,blk(outer,m),ss,router.at[m],to)
                @pl.when(jnp.logical_not(via))
                def _(): act(src,blk(own,m),ss,rown.at[m],to)
        act(obs,obs_out,sobs,robs,place(p,m))
    sends(push)
    other=place(p,jnp.where(b==0,l+1,l-1))
    side=place(p,jnp.where(edge,l,jnp.where(b==0,l-1,l+1)))
    def relation(cs):
        dl=lax.rem(cs-c+Z,Z)
        far=jnp.where(b==0,dl>=Z//2,(dl>=1)&(dl<=Z//2))
        do=lax.rem(cs-jnp.where(b==0,c-1,c+1)+2*Z,Z)
        out_near=jnp.where(b==0,(do>=1)&(do<=Z//2),do>=Z//2)
        return jnp.logical_not(far)|edge, out_near&jnp.logical_not(edge)
    def each(offs=NEAR):
        for off in offs:
            cs=lax.rem(c+off,Z)
            near,onear=relation(cs)
            for e in (0,1): yield near,onear,place(p,2*cs+e)
    def across(start):
        for near,onear,s in each():
            @pl.when(onear)
            def _():
                if start: landed(outer,s,router.at[s])
                k=remote(blk(outer,s),blk(own,s),sfwd.at[s],rown.at[s],side)
                k.start() if start else k.wait_send()
            @pl.when(near)
            def _():
                if start: landed(own,s,rown.at[s])
                k=remote(blk(own,s),blk(inner,s),sin.at[s],rinner.at[s],other)
                k.start() if start else k.wait_send()
            @pl.when(near&jnp.logical_not(edge))
            def _():
                k=remote(blk(own,s),blk(outer,s),sfwd.at[n+s],router.at[s],side)
                k.start() if start else k.wait_send()
            @pl.when(edge&open_)
            def _():
                k=remote(blk(own,s),blk(outer,s),sfwd.at[n+s],router.at[s],m,next_patch)
                k.start() if start else k.wait_send()
    def inside(start):
        for near,onear,s in each():
            @pl.when(jnp.logical_not(near))
            def _():
                if start: landed(own,s,rown.at[s])
                k=remote(blk(own,s),blk(inner,s),sin.at[s],rinner.at[s],other)
                k.start() if start else k.wait_send()
    across(True)
    inside(True)
    for near,onear,s in each():
        @pl.when(jnp.logical_not(onear)&open_)
        def _(): landed(outer,s,router.at[s])
        landed(inner,s,rinner.at[s])
    pltpu.make_async_copy(obs_out,obs_out,robs).wait()
    sends(sent)
    across(False)
    inside(False)

def gather(fc,obs):
    n,B,W=fc.shape; A=pl.BlockSpec(memory_space=pl.ANY); D=pltpu.SemaphoreType.DMA
    o=jax.ShapeDtypeStruct((n*B,W),F32)
    return pl.pallas_call(gather_kernel,out_shape=(o,o,o,jax.ShapeDtypeStruct(obs.shape,F32)),in_specs=[A,A],out_specs=(A,)*4,
        scratch_shapes=[D((n,)),D((2*n,)),D((n,)),D((n,)),D((n,)),D((n,)),D,D],
        compiler_params=pltpu.CompilerParams(collective_id=1,has_side_effects=True),name='gather')(fc,obs)

def scatter_kernel(x_ref, out_ref, ssem, rsem, lsem):
    p=lax.axis_index('patch'); m=lax.axis_index('member'); n=out_ref.shape[0]; B=out_ref.shape[1]; row=place(p,m)
    barrier=pltpu.get_barrier_semaphore()
    for d in range(1,n):
        pl.semaphore_signal(barrier,inc=1,device_id=(p,lax.rem(m+d,n)),device_id_type=MESH)
    own=pltpu.make_async_copy(x_ref.at[pl.ds(pl.multiple_of(m*B,B),B)],out_ref.at[row],lsem)
    own.start()
    pl.semaphore_wait(barrier,n-1)
    cps=[]
    for d in [8,7,9,6,10,5,11,4,12,3,13,2,14,1,15]:
        to=lax.rem(m+d,n)
        c=pltpu.make_async_remote_copy(src_ref=x_ref.at[pl.ds(pl.multiple_of(to*B,B),B)],dst_ref=out_ref.at[row],
            send_sem=ssem.at[d],recv_sem=rsem.at[d],device_id=(p,to),device_id_type=MESH)
        c.start(); cps.append(c)
    own.wait()
    for c in cps: c.wait()
def scatter(x,n=16):
    A=pl.BlockSpec(memory_space=pl.ANY)
    return pl.pallas_call(scatter_kernel,out_shape=jax.ShapeDtypeStruct((n,x.shape[0]//n,x.shape[1]),F32),
      in_specs=[A],out_specs=A,scratch_shapes=[pltpu.SemaphoreType.DMA((n,)),pltpu.SemaphoreType.DMA((n,)),pltpu.SemaphoreType.DMA],
      compiler_params=pltpu.CompilerParams(collective_id=2,has_side_effects=True),name='scatter')(x)


def per_device(
    init_field, flow_fields, emission, observed_cell, observed_count, observed_value, observed_scale
):
    rows = forecast(init_field, flow_fields, emission)
    count = jnp.broadcast_to(observed_count.astype(F32)[:, None], observed_value.shape)
    cells = observed_cell.astype(F32)
    obs = jnp.concatenate([cells, count, observed_value, observed_scale] * 2, axis=0)
    own, outer, inner, obs = gather(rows, obs)
    patch = lax.axis_index("patch")
    line = place(patch, lax.axis_index("member"))
    closed = ((patch == 0) & (line == 0)) | ((patch == lax.axis_size("patch") - 1) & (line == 15))
    flags = jnp.stack([1 - line % 2, 1 - closed.astype(jnp.int32)])
    analysed = solve(flags, own, outer, inner, obs)
    return jnp.transpose(scatter(analysed), (1, 0, 2))


def solution(mesh):
    return jax.shard_map(
        per_device,
        mesh=mesh,
        in_specs=(
            P("member", "patch", None),
            P(None, "patch", None),
            P("member"),
            P(("patch", "member"), None),
            P(("patch", "member")),
            P(("patch", "member"), None),
            P(("patch", "member"), None),
        ),
        out_specs=P("member", "patch", None),
        check_vma=False,
    )
```

```python
import functools
import math

import jax
import jax.numpy as jnp
from jax import lax
from jax.experimental import pallas as pl
from jax.experimental.pallas import tpu as pltpu
from jax.sharding import PartitionSpec as P

F32=jnp.float32; BF=jnp.bfloat16
HIGH=lax.Precision.HIGHEST
NT=(((1,),(1,)),((),())); TN=(((0,),(0,)),((),())); NN=(((1,),(0,)),((),()))
def bdot(a,b,dims): return lax.dot_general(a,b,dims,preferred_element_type=F32)
def split2(x):
    hi=x.astype(BF); lo=(x-hi.astype(F32)).astype(BF)
    return hi,lo

def tree(terms):
    while len(terms)>1:
        terms=[terms[a]+terms[a+1] if a+1<len(terms) else terms[a] for a in range(0,len(terms),2)]
    return terms[0]

def leaf_inverse(rows):
    G=len(rows); full=(8,128)
    lane=lax.broadcasted_iota(jnp.int32,full,1)
    sub=lax.broadcasted_iota(jnp.int32,full,0)
    down=lambda x,i: jnp.broadcast_to(x[i:i+1,:],full)
    for t in range(G):
        across=lambda g,j: jnp.broadcast_to(rows[g][:,8*t+j:8*t+j+1],full)
        inside=(lane>=8*t)&(lane<8*t+8)
        c=[across(t,j) for j in range(8)]
        src=[jnp.where(inside,jnp.where(lane==8*t+i,1.0,0.0),down(rows[t],i)) for i in range(8)]
        for p in range(8):
            r=1.0/down(c[p],p)
            at=sub==p
            mult=c[p]
            for j in range(8):
                if j==p: continue
                x=down(c[j],p)*r
                c[j]=jnp.where(at,x,c[j]-mult*x)
            c[p]=jnp.where(at,r,-(mult*r))
        new=tree([c[j]*src[j] for j in range(8)])
        rep=[down(new,i) for i in range(8)]
        out=[]
        for g in range(G):
            if g==t:
                out.append(new)
            else:
                out.append(jnp.where(inside,0.0,rows[g])-tree([across(g,i)*rep[i] for i in range(8)]))
        rows=out
    return rows

def solve_kernel(own_ref, outer_ref, inner_ref, obs_ref, out_ref,
                 ahi, alo, gt_ref, shi, slo, T):
    members=own_ref.shape[0]; W=own_ref.shape[1]; C=3*W; SL=obs_ref.shape[1]
    root=math.sqrt(members-1)
    patch=lax.axis_index('patch'); line=place(patch,lax.axis_index('member'))
    even=lax.rem(line,2)==0; closed=((patch==0)&(line==0))|((patch==lax.axis_size('patch')-1)&(line==15))
    j=lax.broadcasted_iota(jnp.int32,(1,SL),1)
    obs=obs_ref[...]
    act=jnp.where(j.astype(F32)<obs[1:2],1.0,0.0).astype(F32)
    w=act*obs[3:4]; w2=w*w; w2v=w2*obs[2:3]
    def split3(x):
        a=x.astype(BF).astype(F32); x=x-a; b=x.astype(BF).astype(F32); return a,b,x-b
    a0,a1,a2=split3(w2); b0,b1,b2=split3(w2v)
    lhs=jnp.concatenate([a0,a1,a2,b0,b1,b2,act,jnp.zeros_like(act)],axis=0).astype(BF)
    cell=obs[0:1].astype(jnp.int32)
    swapped=jnp.where(cell<W,cell+2*W,jnp.where(cell<2*W,cell,cell-2*W))
    cell=jnp.where(even,cell,swapped)
    et=(lax.broadcasted_iota(jnp.int32,(C,SL),0)==cell).astype(F32).astype(BF)
    sums=bdot(lhs,et,NT)
    lam=sums[0:1]+sums[1:2]+sums[2:3]
    bet=sums[3:4]+sums[4:5]+sums[5:6]
    present=sums[6:7]>0.5
    pres8=jnp.broadcast_to(jnp.where(present,1.0,0.0),(8,C)).astype(BF)
    tri=(lax.broadcasted_iota(jnp.int32,(C,C),0)<=lax.broadcasted_iota(jnp.int32,(C,C),1)).astype(F32).astype(BF)
    rank=bdot(pres8,tri,NN)[0:1]
    slot=jnp.where(present,rank-1.0,-1.0).astype(jnp.int32)
    gt_ref[...]=(lax.broadcasted_iota(jnp.int32,(SL,C),0)==slot).astype(F32).astype(BF)
    s=jnp.sqrt(lam)
    mus=[]
    for q,ref in enumerate((outer_ref,own_ref,inner_ref)):
        x=ref[...]
        if q==0: x=jnp.where(closed,0.0,x)
        mu=jnp.sum(x,axis=0,keepdims=True)*(1.0/members)
        mus.append(mu)
        sl=slice(q*W,(q+1)*W)
        h,l=split2((x-mu)*(s[:,sl]*(1.0/root)))
        ahi[:,sl]=h; alo[:,sl]=l
    mu=jnp.concatenate(mus,axis=1)
    d=jnp.where(present,(bet-lam*mu)/jnp.where(present,s,1.0),0.0)*(1.0/root)
    gt=gt_ref[...]
    shi[...]=bdot(gt,ahi[...],NT).astype(BF)
    slo[...]=bdot(gt,alo[...],NT).astype(BF)
    h,l=shi[...],slo[...]
    eye=(lax.broadcasted_iota(jnp.int32,(SL,SL),0)==lax.broadcasted_iota(jnp.int32,(SL,SL),1)).astype(F32)
    T[:,0:SL]=eye+bdot(h,h,NT)+(bdot(h,l,NT)+bdot(l,h,NT))
    oh,ol=split2(own_ref[...]-mus[1])
    T[:,SL:]=bdot(h,oh,NN)+(bdot(h,ol,NN)+bdot(l,oh,NN))
    total=jnp.max(rank)
    def step(k):
        o=k*128
        rows=leaf_inverse([T[o+8*g:o+8*g+8,o:o+128] for g in range(16)])
        dinv=jnp.concatenate(rows,axis=0)
        cuts=[(o+128,o+256),(o+256,SL+W)] if o+128<SL else [(SL,SL+W)]
        for lo,hi in cuts:
            U=jnp.dot(dinv,T[o:o+128,lo:hi],precision=HIGH,preferred_element_type=F32)
            T[o:o+128,lo:hi]=U
            order=[i for i in range(SL//128) if i!=k]
            order=[i for i in order if i>k]+[i for i in order if i<k]
            for i in order:
                T[i*128:i*128+128,lo:hi]=T[i*128:i*128+128,lo:hi]-jnp.dot(T[i*128:i*128+128,o:o+128],U,precision=HIGH,preferred_element_type=F32)
    for k in range(3): step(k)
    @pl.when(total>384.5)
    def _(): step(3)
    yh,yl=split2(T[:,SL:])
    zh=bdot(gt,yh,TN); zl=bdot(gt,yl,TN)
    off=jnp.dot(jnp.broadcast_to(d,(8,C)),zh+zl,precision=HIGH,preferred_element_type=F32)[0:1]
    zh=zh.astype(BF); zl=zl.astype(BF)
    sy=bdot(ahi[...],zh,NN)+(bdot(ahi[...],zl,NN)+bdot(alo[...],zh,NN))
    out_ref[...]=own_ref[...]-0.5*sy+off

def solve(own,outer,inner,obs):
    m,W=own.shape; SL=obs.shape[1]; C=3*W
    V=pl.BlockSpec(memory_space=pltpu.VMEM)
    return pl.pallas_call(solve_kernel,out_shape=jax.ShapeDtypeStruct((m,W),F32),in_specs=[V,V,V,V],out_specs=V,
        scratch_shapes=[pltpu.VMEM((m,C),BF),pltpu.VMEM((m,C),BF),pltpu.VMEM((SL,C),BF),pltpu.VMEM((SL,m),BF),pltpu.VMEM((SL,m),BF),
                        pltpu.VMEM((SL,SL+W),F32)],
        compiler_params=pltpu.CompilerParams(vmem_limit_bytes=40<<20),name='solve')(own,outer,inner,obs)


MESH=pl.DeviceIdType.MESH

def forecast_kernel(count_ref, x_ref, fl_hbm, em_hbm, cell_hbm, value_hbm, scale_hbm, out_ref, obs_ref, xa, xb, fl_ref, em_ref, cell_ref, value_ref, scale_ref, fb, g1, flx, sbuf, rbuf, ssem, rsem, lsem):
    P_=lax.axis_size('patch'); p=lax.axis_index('patch'); m=lax.axis_index('member')
    Bn=em_ref.shape[1]; R=x_ref.shape[0]//Bn; W=x_ref.shape[1]
    loads=[pltpu.make_async_copy(x_ref.at[:,h*128:(h+1)*128],t,lsem.at[h]) for h,t in enumerate((xa,xb))]
    small=[pltpu.make_async_copy(a,t,lsem.at[2+i]) for i,(a,t) in enumerate(((fl_hbm,fl_ref),(em_hbm,em_ref),(cell_hbm,cell_ref),(value_hbm,value_ref),(scale_hbm,scale_ref)))]
    for c in loads+small: c.start()
    barrier=pltpu.get_barrier_semaphore()
    up,dn=lax.rem(p+1,P_),lax.rem(p+P_-1,P_)
    for q in (up,dn): pl.semaphore_signal(barrier,inc=1,device_id=(q,m),device_id_type=MESH)
    row=lambda r: jnp.concatenate([t[pl.ds(r,Bn,stride=R),:] for t in (xa,xb)],axis=1)
    for c in loads+small[:2]: c.wait()
    for i in range(2):
        sbuf[0,i*Bn:(i+1)*Bn]=row(i)
        sbuf[1,i*Bn:(i+1)*Bn]=row(R-2+i)
    for f in range(4):
        sbuf[0,2*Bn+2*f:2*Bn+2*f+2]=fl_ref[f,0:2]
        sbuf[1,2*Bn+2*f:2*Bn+2*f+2]=fl_ref[f,R-2:R]
    pl.semaphore_wait(barrier,2)
    cps=[]
    for k,q in ((0,dn),(1,up)):
        c=pltpu.make_async_remote_copy(src_ref=sbuf.at[k],dst_ref=rbuf.at[k],send_sem=ssem.at[k],recv_sem=rsem.at[k],device_id=(q,m),device_id_type=MESH)
        c.start(); cps.append(c)
    eye=lax.broadcasted_iota(jnp.int32,(Bn,Bn),0)==lax.broadcasted_iota(jnp.int32,(Bn,Bn),1)
    em=jnp.sum(jnp.where(eye,jnp.broadcast_to(em_ref[...],(Bn,Bn)),0.0),axis=1,keepdims=True)
    emb=jnp.broadcast_to(em,(Bn,W))
    for f in range(4): flx[f,2:2+R]=fl_ref[f]
    for r in range(R): fb[r+2]=row(r)
    mlo=jnp.where(p>0,1.0,0.0); mhi=jnp.where(p<P_-1,1.0,0.0)
    def step(f,b,a,i):
        rf=flx[0,pl.ds(i,1),:]; cf=flx[1,pl.ds(i,1),:]; dc=flx[2,pl.ds(i,1),:]; so=flx[3,pl.ds(i,1),:]
        bc=pltpu.roll(f,1,1); ac=pltpu.roll(f,W-1,1)
        adv=(f-jnp.maximum(rf,0.0)*(f-b)-jnp.minimum(rf,0.0)*(a-f)-jnp.maximum(cf,0.0)*(f-bc)-jnp.minimum(cf,0.0)*(ac-f))
        return (1.0-dc)*adv+emb*so
    def first(r,mask=None):
        v=step(fb[r+2],fb[r+1],fb[r+3],r+2)
        g1[r+1]=v if mask is None else v*mask
    def second(r):
        out_ref[r]=step(g1[r+1],g1[r],g1[r+2],r+2)
    for c in small[2:]: c.wait()
    SL=obs_ref.shape[1]
    for i in (0,4):
        obs_ref[i:i+1]=cell_ref[...].astype(F32)
        obs_ref[i+1:i+2]=jnp.broadcast_to(count_ref[0].astype(F32),(1,SL))
        obs_ref[i+2:i+3]=value_ref[...]
        obs_ref[i+3:i+4]=scale_ref[...]
    lax.fori_loop(1,R-1,lambda r,_:(first(r),0)[1],0)
    lax.fori_loop(2,R-2,lambda r,_:(second(r),0)[1],0)
    for c in cps: c.wait()
    for i in range(2):
        fb[i]=rbuf[1,i*Bn:(i+1)*Bn]*mlo
        fb[R+2+i]=rbuf[0,i*Bn:(i+1)*Bn]*mhi
    for f in range(4):
        flx[f,0:2]=rbuf[1,2*Bn+2*f:2*Bn+2*f+2]
        flx[f,R+2:R+4]=rbuf[0,2*Bn+2*f:2*Bn+2*f+2]
    for r,k in ((-1,mlo),(0,None),(R-1,None),(R,mhi)): first(r,k)
    for r in (0,1,R-2,R-1): second(r)

def forecast(x,fl,em,cells,count,values,scales):
    Bn,R,W=x.shape; V=pl.BlockSpec(memory_space=pltpu.VMEM); A=pl.BlockSpec(memory_space=pltpu.HBM); D=pltpu.SemaphoreType.DMA
    H=2*Bn+8; SL=cells.shape[1]; S=lambda *shape: pltpu.VMEM(shape,F32)
    return pl.pallas_call(forecast_kernel,out_shape=(jax.ShapeDtypeStruct((R,Bn,W),F32),jax.ShapeDtypeStruct((8,SL),F32)),
        in_specs=[pl.BlockSpec(memory_space=pltpu.SMEM)]+[A]*6,out_specs=(V,V),
        scratch_shapes=[S(Bn*R,128),S(Bn*R,128),S(4,R,W),S(1,Bn),pltpu.VMEM((1,SL),jnp.int32),S(1,SL),S(1,SL),S(R+4,Bn,W),S(R+2,Bn,W),S(4,R+8,W),S(2,H,W),S(2,H,W),
                        D((2,)),D((2,)),D((7,))],
        compiler_params=pltpu.CompilerParams(collective_id=0,has_side_effects=True,vmem_limit_bytes=16<<20),name='forecast')(count,*(pltpu.with_memory_space_constraint(a,pltpu.HBM) for a in (x.reshape(Bn*R,W),fl,em.reshape(1,Bn),cells,values,scales)))

def place(p,l):
    return jnp.where(lax.rem(p,2)==0,l,15-l)

def gather_kernel(fc, obs, own, outer, inner, obs_out, ssend, sfwd, sin, rown, router, rinner, sobs, robs):
    n=16
    P_=lax.axis_size('patch'); p=lax.axis_index('patch'); m=lax.axis_index('member')
    B=fc.shape[1]; Z=n//2
    l=place(p,m); c=l//2; b=lax.rem(l,2)
    first=(b==0)&(c==0); last=(b==1)&(c==Z-1); edge=first|last
    open_=jnp.logical_not((first&(p==0))|(last&(p==P_-1)))
    next_patch=jnp.where(first,p-1,p+1)
    barrier=pltpu.get_barrier_semaphore()
    for d in range(1,n):
        pl.semaphore_signal(barrier,inc=1,device_id=(p,lax.rem(m+d,n)),device_id_type=MESH)
    @pl.when(edge&open_)
    def _():
        pl.semaphore_signal(barrier,inc=1,device_id=(next_patch,m),device_id_type=MESH)
        pl.semaphore_wait(barrier,n)
    @pl.when(jnp.logical_not(edge&open_))
    def _(): pl.semaphore_wait(barrier,n-1)
    blk=lambda ref,s: ref.at[pl.ds(pl.multiple_of(s*B,B),B)]
    def remote(src,dst,ss,rs,to,tp=None):
        return pltpu.make_async_remote_copy(src_ref=src,dst_ref=dst,send_sem=ss,recv_sem=rs,device_id=(p if tp is None else tp,to),device_id_type=MESH)
    def push(src,dst,ss,rs,to):
        @pl.when(to==m)
        def _(): pltpu.make_async_copy(src,dst,rs).start()
        @pl.when(to!=m)
        def _(): remote(src,dst,ss,rs,to).start()
    def sent(src,dst,ss,rs,to):
        @pl.when(to!=m)
        def _(): remote(src,dst,ss,rs,to).wait_send()
    def landed(ref,s,rs):
        d=blk(ref,s); pltpu.make_async_copy(d,d,rs).wait()
    def even_row(cr):
        dl=lax.rem(c-cr+Z,Z); left=(dl>=Z//2)&(cr>0)
        return left, place(p,jnp.where(left,2*cr-1,2*cr))
    def odd_row(cr):
        dl=lax.rem(c-cr+Z,Z); right=(dl>=1)&(dl<=Z//2)&(cr<Z-1)
        return right, place(p,jnp.where(right,2*cr+2,2*cr+1))
    NEAR=[0,1,7,2,6,3,5,4]
    def sends(act):
        for off in NEAR:
            cr=lax.rem(c+off,Z)
            for odd in (0,1):
                via,to=(odd_row if odd else even_row)(cr)
                r=2*cr+odd
                src=fc.at[r]; ss=ssend.at[r]
                @pl.when(via)
                def _(): act(src,blk(outer,m),ss,router.at[m],to)
                @pl.when(jnp.logical_not(via))
                def _(): act(src,blk(own,m),ss,rown.at[m],to)
        act(obs,obs_out,sobs,robs,place(p,m))
    sends(push)
    other=place(p,jnp.where(b==0,l+1,l-1))
    side=place(p,jnp.where(edge,l,jnp.where(b==0,l-1,l+1)))
    def relation(cs):
        dl=lax.rem(cs-c+Z,Z)
        far=jnp.where(b==0,dl>=Z//2,(dl>=1)&(dl<=Z//2))
        do=lax.rem(cs-jnp.where(b==0,c-1,c+1)+2*Z,Z)
        out_near=jnp.where(b==0,(do>=1)&(do<=Z//2),do>=Z//2)
        return jnp.logical_not(far)|edge, out_near&jnp.logical_not(edge)
    def each(offs=NEAR):
        for off in offs:
            cs=lax.rem(c+off,Z)
            near,onear=relation(cs)
            for e in (0,1): yield near,onear,place(p,2*cs+e)
    def across(start):
        for near,onear,s in each():
            @pl.when(onear)
            def _():
                if start: landed(outer,s,router.at[s])
                k=remote(blk(outer,s),blk(own,s),sfwd.at[s],rown.at[s],side)
                k.start() if start else k.wait_send()
            @pl.when(near)
            def _():
                if start: landed(own,s,rown.at[s])
                k=remote(blk(own,s),blk(inner,s),sin.at[s],rinner.at[s],other)
                k.start() if start else k.wait_send()
            @pl.when(near&jnp.logical_not(edge))
            def _():
                k=remote(blk(own,s),blk(outer,s),sfwd.at[n+s],router.at[s],side)
                k.start() if start else k.wait_send()
            @pl.when(edge&open_)
            def _():
                k=remote(blk(own,s),blk(outer,s),sfwd.at[n+s],router.at[s],m,next_patch)
                k.start() if start else k.wait_send()
    def inside(start):
        for near,onear,s in each():
            @pl.when(jnp.logical_not(near))
            def _():
                if start: landed(own,s,rown.at[s])
                k=remote(blk(own,s),blk(inner,s),sin.at[s],rinner.at[s],other)
                k.start() if start else k.wait_send()
    across(True)
    inside(True)
    for near,onear,s in each():
        @pl.when(jnp.logical_not(onear)&open_)
        def _(): landed(outer,s,router.at[s])
        landed(inner,s,rinner.at[s])
    pltpu.make_async_copy(obs_out,obs_out,robs).wait()
    sends(sent)
    across(False)
    inside(False)

def gather(fc,obs):
    n,B,W=fc.shape; A=pl.BlockSpec(memory_space=pltpu.VMEM); D=pltpu.SemaphoreType.DMA
    o=jax.ShapeDtypeStruct((n*B,W),F32)
    return pl.pallas_call(gather_kernel,out_shape=(o,o,o,jax.ShapeDtypeStruct(obs.shape,F32)),in_specs=[A,A],out_specs=(A,)*4,
        scratch_shapes=[D((n,)),D((2*n,)),D((n,)),D((n,)),D((n,)),D((n,)),D,D],
        compiler_params=pltpu.CompilerParams(collective_id=1,has_side_effects=True,vmem_limit_bytes=16<<20),name='gather')(fc,obs)

def scatter_kernel(x_ref, out_ref, ssem, rsem, lsem):
    p=lax.axis_index('patch'); m=lax.axis_index('member'); n=out_ref.shape[0]; B=out_ref.shape[1]; row=place(p,m)
    barrier=pltpu.get_barrier_semaphore()
    for d in range(1,n):
        pl.semaphore_signal(barrier,inc=1,device_id=(p,lax.rem(m+d,n)),device_id_type=MESH)
    own=pltpu.make_async_copy(x_ref.at[pl.ds(pl.multiple_of(m*B,B),B)],out_ref.at[row],lsem)
    own.start()
    pl.semaphore_wait(barrier,n-1)
    cps=[]
    for d in [8,7,9,6,10,5,11,4,12,3,13,2,14,1,15]:
        to=lax.rem(m+d,n)
        c=pltpu.make_async_remote_copy(src_ref=x_ref.at[pl.ds(pl.multiple_of(to*B,B),B)],dst_ref=out_ref.at[row],
            send_sem=ssem.at[d],recv_sem=rsem.at[d],device_id=(p,to),device_id_type=MESH)
        c.start(); cps.append(c)
    own.wait()
    for c in cps: c.wait()
def scatter(x,n=16):
    A=pl.BlockSpec(memory_space=pltpu.VMEM)
    return pl.pallas_call(scatter_kernel,out_shape=jax.ShapeDtypeStruct((n,x.shape[0]//n,x.shape[1]),F32),
      in_specs=[A],out_specs=A,scratch_shapes=[pltpu.SemaphoreType.DMA((n,)),pltpu.SemaphoreType.DMA((n,)),pltpu.SemaphoreType.DMA],
      compiler_params=pltpu.CompilerParams(collective_id=2,has_side_effects=True,vmem_limit_bytes=16<<20),name='scatter')(x)


def per_device(
    init_field, flow_fields, emission, observed_cell, observed_count, observed_value, observed_scale
):
    rows, obs = forecast(
        init_field, flow_fields, emission, observed_cell, observed_count, observed_value, observed_scale
    )
    analysed = solve(*gather(rows, obs))
    return jnp.transpose(scatter(analysed), (1, 0, 2))


def solution(mesh):
    return jax.shard_map(
        per_device,
        mesh=mesh,
        in_specs=(
            P("member", "patch", None),
            P(None, "patch", None),
            P("member"),
            P(("patch", "member"), None),
            P(("patch", "member")),
            P(("patch", "member"), None),
            P(("patch", "member"), None),
        ),
        out_specs=P("member", "patch", None),
        check_vma=False,
    )
```

```python
import functools
import math

import jax
import jax.numpy as jnp
from jax import lax
from jax.experimental import pallas as pl
from jax.experimental.pallas import tpu as pltpu
from jax.sharding import PartitionSpec as P

F32=jnp.float32; BF=jnp.bfloat16
HIGH=lax.Precision.HIGHEST
NT=(((1,),(1,)),((),())); TN=(((0,),(0,)),((),())); NN=(((1,),(0,)),((),()))
def bdot(a,b,dims): return lax.dot_general(a,b,dims,preferred_element_type=F32)
def split2(x):
    hi=x.astype(BF); lo=(x-hi.astype(F32)).astype(BF)
    return hi,lo

def tree(terms):
    while len(terms)>1:
        terms=[terms[a]+terms[a+1] if a+1<len(terms) else terms[a] for a in range(0,len(terms),2)]
    return terms[0]

def leaf_inverse(rows):
    G=len(rows); full=(8,128)
    lane=lax.broadcasted_iota(jnp.int32,full,1)
    sub=lax.broadcasted_iota(jnp.int32,full,0)
    down=lambda x,i: jnp.broadcast_to(x[i:i+1,:],full)
    for t in range(G):
        across=lambda g,j: jnp.broadcast_to(rows[g][:,8*t+j:8*t+j+1],full)
        inside=(lane>=8*t)&(lane<8*t+8)
        c=[across(t,j) for j in range(8)]
        src=[jnp.where(inside,jnp.where(lane==8*t+i,1.0,0.0),down(rows[t],i)) for i in range(8)]
        for p in range(8):
            r=1.0/down(c[p],p)
            at=sub==p
            mult=c[p]
            for j in range(8):
                if j==p: continue
                x=down(c[j],p)*r
                c[j]=jnp.where(at,x,c[j]-mult*x)
            c[p]=jnp.where(at,r,-(mult*r))
        new=tree([c[j]*src[j] for j in range(8)])
        rep=[down(new,i) for i in range(8)]
        out=[]
        for g in range(G):
            if g==t:
                out.append(new)
            else:
                out.append(jnp.where(inside,0.0,rows[g])-tree([across(g,i)*rep[i] for i in range(8)]))
        rows=out
    return rows

def solve_kernel(own_ref, outer_ref, inner_ref, obs_ref, out_ref,
                 ahi, alo, gt_ref, shi, slo, T):
    members=own_ref.shape[0]; W=own_ref.shape[1]; C=3*W; SL=obs_ref.shape[1]
    root=math.sqrt(members-1)
    patch=lax.axis_index('patch'); line=place(patch,lax.axis_index('member'))
    even=lax.rem(line,2)==0; closed=((patch==0)&(line==0))|((patch==lax.axis_size('patch')-1)&(line==15))
    j=lax.broadcasted_iota(jnp.int32,(1,SL),1)
    obs=obs_ref[...]
    act=jnp.where(j.astype(F32)<obs[1:2],1.0,0.0).astype(F32)
    w=act*obs[3:4]; w2=w*w; w2v=w2*obs[2:3]
    def split3(x):
        a=x.astype(BF).astype(F32); x=x-a; b=x.astype(BF).astype(F32); return a,b,x-b
    a0,a1,a2=split3(w2); b0,b1,b2=split3(w2v)
    lhs=jnp.concatenate([a0,a1,a2,b0,b1,b2,act,jnp.zeros_like(act)],axis=0).astype(BF)
    cell=obs[0:1].astype(jnp.int32)
    swapped=jnp.where(cell<W,cell+2*W,jnp.where(cell<2*W,cell,cell-2*W))
    cell=jnp.where(even,cell,swapped)
    et=(lax.broadcasted_iota(jnp.int32,(C,SL),0)==cell).astype(F32).astype(BF)
    sums=bdot(lhs,et,NT)
    lam=sums[0:1]+sums[1:2]+sums[2:3]
    bet=sums[3:4]+sums[4:5]+sums[5:6]
    present=sums[6:7]>0.5
    pres8=jnp.broadcast_to(jnp.where(present,1.0,0.0),(8,C)).astype(BF)
    tri=(lax.broadcasted_iota(jnp.int32,(C,C),0)<=lax.broadcasted_iota(jnp.int32,(C,C),1)).astype(F32).astype(BF)
    rank=bdot(pres8,tri,NN)[0:1]
    slot=jnp.where(present,rank-1.0,-1.0).astype(jnp.int32)
    gt_ref[...]=(lax.broadcasted_iota(jnp.int32,(SL,C),0)==slot).astype(F32).astype(BF)
    s=jnp.sqrt(lam)
    mus=[]
    for q,ref in enumerate((outer_ref,own_ref,inner_ref)):
        x=ref[...]
        if q==0: x=jnp.where(closed,0.0,x)
        mu=jnp.sum(x,axis=0,keepdims=True)*(1.0/members)
        mus.append(mu)
        sl=slice(q*W,(q+1)*W)
        h,l=split2((x-mu)*(s[:,sl]*(1.0/root)))
        ahi[:,sl]=h; alo[:,sl]=l
    mu=jnp.concatenate(mus,axis=1)
    d=jnp.where(present,(bet-lam*mu)/jnp.where(present,s,1.0),0.0)*(1.0/root)
    gt=gt_ref[...]
    shi[...]=bdot(gt,ahi[...],NT).astype(BF)
    slo[...]=bdot(gt,alo[...],NT).astype(BF)
    h,l=shi[...],slo[...]
    eye=(lax.broadcasted_iota(jnp.int32,(SL,SL),0)==lax.broadcasted_iota(jnp.int32,(SL,SL),1)).astype(F32)
    T[:,0:SL]=eye+bdot(h,h,NT)+(bdot(h,l,NT)+bdot(l,h,NT))
    oh,ol=split2(own_ref[...]-mus[1])
    T[:,SL:]=bdot(h,oh,NN)+(bdot(h,ol,NN)+bdot(l,oh,NN))
    total=jnp.max(rank)
    def step(k):
        o=k*128
        rows=leaf_inverse([T[o+8*g:o+8*g+8,o:o+128] for g in range(16)])
        dinv=jnp.concatenate(rows,axis=0)
        cuts=[(o+128,o+256),(o+256,SL+W)] if o+128<SL else [(SL,SL+W)]
        for lo,hi in cuts:
            U=jnp.dot(dinv,T[o:o+128,lo:hi],precision=HIGH,preferred_element_type=F32)
            T[o:o+128,lo:hi]=U
            order=[i for i in range(SL//128) if i!=k]
            order=[i for i in order if i>k]+[i for i in order if i<k]
            for i in order:
                T[i*128:i*128+128,lo:hi]=T[i*128:i*128+128,lo:hi]-jnp.dot(T[i*128:i*128+128,o:o+128],U,precision=HIGH,preferred_element_type=F32)
    for k in range(3): step(k)
    @pl.when(total>384.5)
    def _(): step(3)
    yh,yl=split2(T[:,SL:])
    zh=bdot(gt,yh,TN); zl=bdot(gt,yl,TN)
    off=jnp.dot(jnp.broadcast_to(d,(8,C)),zh+zl,precision=HIGH,preferred_element_type=F32)[0:1]
    zh=zh.astype(BF); zl=zl.astype(BF)
    sy=bdot(ahi[...],zh,NN)+(bdot(ahi[...],zl,NN)+bdot(alo[...],zh,NN))
    out_ref[...]=own_ref[...]-0.5*sy+off

def solve(own,outer,inner,obs):
    m,W=own.shape; SL=obs.shape[1]; C=3*W
    V=pl.BlockSpec(memory_space=pltpu.VMEM)
    return pl.pallas_call(solve_kernel,out_shape=jax.ShapeDtypeStruct((m,W),F32),in_specs=[V,V,V,V],out_specs=V,
        scratch_shapes=[pltpu.VMEM((m,C),BF),pltpu.VMEM((m,C),BF),pltpu.VMEM((SL,C),BF),pltpu.VMEM((SL,m),BF),pltpu.VMEM((SL,m),BF),
                        pltpu.VMEM((SL,SL+W),F32)],
        compiler_params=pltpu.CompilerParams(vmem_limit_bytes=40<<20),name='solve')(own,outer,inner,obs)


MESH=pl.DeviceIdType.MESH

def place(p,l):
    return jnp.where(lax.rem(p,2)==0,l,15-l)

def front_kernel(count_ref, x_ref, fl_hbm, em_hbm, cell_hbm, value_hbm, scale_hbm, own, outer, inner, obs_out, fc, obs, xa, xb, fl_ref, em_ref, cell_ref, value_ref, scale_ref, fb, g1, flx, sbuf, rbuf, hsend, hrecv, lsem, ssend, sfwd, sin, rown, router, rinner, sobs, robs):
    n=16; Z=n//2
    P_=lax.axis_size('patch'); p=lax.axis_index('patch'); m=lax.axis_index('member')
    Bn=em_ref.shape[1]; R=x_ref.shape[0]//Bn; W=x_ref.shape[1]
    loads=[pltpu.make_async_copy(x_ref.at[:,h*128:(h+1)*128],t,lsem.at[h]) for h,t in enumerate((xa,xb))]
    small=[pltpu.make_async_copy(a,t,lsem.at[2+i]) for i,(a,t) in enumerate(((fl_hbm,fl_ref),(em_hbm,em_ref),(cell_hbm,cell_ref),(value_hbm,value_ref),(scale_hbm,scale_ref)))]
    for c in loads+small: c.start()
    barrier=pltpu.get_barrier_semaphore()
    up,dn=lax.rem(p+1,P_),lax.rem(p+P_-1,P_)
    for q in (up,dn): pl.semaphore_signal(barrier,inc=1,device_id=(q,m),device_id_type=MESH)
    for d in range(1,n):
        pl.semaphore_signal(barrier,inc=1,device_id=(p,lax.rem(m+d,n)),device_id_type=MESH)
    row=lambda r: jnp.concatenate([t[pl.ds(r,Bn,stride=R),:] for t in (xa,xb)],axis=1)
    for c in loads+small[:2]: c.wait()
    for i in range(2):
        sbuf[0,i*Bn:(i+1)*Bn]=row(i)
        sbuf[1,i*Bn:(i+1)*Bn]=row(R-2+i)
    for f in range(4):
        sbuf[0,2*Bn+2*f:2*Bn+2*f+2]=fl_ref[f,0:2]
        sbuf[1,2*Bn+2*f:2*Bn+2*f+2]=fl_ref[f,R-2:R]
    pl.semaphore_wait(barrier,n+1)
    cps=[]
    for k,q in ((0,dn),(1,up)):
        c=pltpu.make_async_remote_copy(src_ref=sbuf.at[k],dst_ref=rbuf.at[k],send_sem=hsend.at[k],recv_sem=hrecv.at[k],device_id=(q,m),device_id_type=MESH)
        c.start(); cps.append(c)
    eye=lax.broadcasted_iota(jnp.int32,(Bn,Bn),0)==lax.broadcasted_iota(jnp.int32,(Bn,Bn),1)
    em=jnp.sum(jnp.where(eye,jnp.broadcast_to(em_ref[...],(Bn,Bn)),0.0),axis=1,keepdims=True)
    emb=jnp.broadcast_to(em,(Bn,W))
    for f in range(4): flx[f,2:2+R]=fl_ref[f]
    for r in range(R): fb[r+2]=row(r)
    mlo=jnp.where(p>0,1.0,0.0); mhi=jnp.where(p<P_-1,1.0,0.0)
    def step(f,b,a,i):
        rf=flx[0,pl.ds(i,1),:]; cf=flx[1,pl.ds(i,1),:]; dc=flx[2,pl.ds(i,1),:]; so=flx[3,pl.ds(i,1),:]
        bc=pltpu.roll(f,1,1); ac=pltpu.roll(f,W-1,1)
        adv=(f-jnp.maximum(rf,0.0)*(f-b)-jnp.minimum(rf,0.0)*(a-f)-jnp.maximum(cf,0.0)*(f-bc)-jnp.minimum(cf,0.0)*(ac-f))
        return (1.0-dc)*adv+emb*so
    def once(r,mask=None):
        v=step(fb[r+2],fb[r+1],fb[r+3],r+2)
        g1[r+1]=v if mask is None else v*mask
    def second(r):
        fc[r]=step(g1[r+1],g1[r],g1[r+2],r+2)
    for c in small[2:]: c.wait()
    SL=obs.shape[1]
    for i in (0,4):
        obs[i:i+1]=cell_ref[...].astype(F32)
        obs[i+1:i+2]=jnp.broadcast_to(count_ref[0].astype(F32),(1,SL))
        obs[i+2:i+3]=value_ref[...]
        obs[i+3:i+4]=scale_ref[...]
    lax.fori_loop(1,R-1,lambda r,_:(once(r),0)[1],0)
    lax.fori_loop(2,R-2,lambda r,_:(second(r),0)[1],0)
    B=Bn
    l=place(p,m); c=l//2; b=lax.rem(l,2)
    first=(b==0)&(c==0); last=(b==1)&(c==Z-1); edge=first|last
    open_=jnp.logical_not((first&(p==0))|(last&(p==P_-1)))
    next_patch=jnp.where(first,p-1,p+1)
    blk=lambda ref,s: ref.at[pl.ds(pl.multiple_of(s*B,B),B)]
    def remote(src,dst,ss,rs,to,tp=None):
        return pltpu.make_async_remote_copy(src_ref=src,dst_ref=dst,send_sem=ss,recv_sem=rs,device_id=(p if tp is None else tp,to),device_id_type=MESH)
    def push(src,dst,ss,rs,to):
        @pl.when(to==m)
        def _(): pltpu.make_async_copy(src,dst,rs).start()
        @pl.when(to!=m)
        def _(): remote(src,dst,ss,rs,to).start()
    def sent(src,dst,ss,rs,to):
        @pl.when(to!=m)
        def _(): remote(src,dst,ss,rs,to).wait_send()
    def landed(ref,s,rs):
        d=blk(ref,s); pltpu.make_async_copy(d,d,rs).wait()
    def even_row(cr):
        dl=lax.rem(c-cr+Z,Z); left=(dl>=Z//2)&(cr>0)
        return left, place(p,jnp.where(left,2*cr-1,2*cr))
    def odd_row(cr):
        dl=lax.rem(c-cr+Z,Z); right=(dl>=1)&(dl<=Z//2)&(cr<Z-1)
        return right, place(p,jnp.where(right,2*cr+2,2*cr+1))
    NEAR=[0,1,7,2,6,3,5,4]
    def sends(act,ends):
        for off in NEAR:
            cr=lax.rem(c+off,Z); due=((cr==0)|(cr==Z-1)) if ends else ((cr>0)&(cr<Z-1))
            for odd in (0,1):
                via,to=(odd_row if odd else even_row)(cr)
                r=2*cr+odd
                src=fc.at[r]; ss=ssend.at[r]
                @pl.when(via&due)
                def _(): act(src,blk(outer,m),ss,router.at[m],to)
                @pl.when(jnp.logical_not(via)&due)
                def _(): act(src,blk(own,m),ss,rown.at[m],to)
        if not ends: act(obs,obs_out,sobs,robs,place(p,m))
    sends(push,False)
    for k_ in cps: k_.wait()
    for i in range(2):
        fb[i]=rbuf[1,i*Bn:(i+1)*Bn]*mlo
        fb[R+2+i]=rbuf[0,i*Bn:(i+1)*Bn]*mhi
    for f in range(4):
        flx[f,0:2]=rbuf[1,2*Bn+2*f:2*Bn+2*f+2]
        flx[f,R+2:R+4]=rbuf[0,2*Bn+2*f:2*Bn+2*f+2]
    for r,k in ((-1,mlo),(0,None),(R-1,None),(R,mhi)): once(r,k)
    for r in (0,1,R-2,R-1): second(r)

    sends(push,True)
    other=place(p,jnp.where(b==0,l+1,l-1))
    side=place(p,jnp.where(edge,l,jnp.where(b==0,l-1,l+1)))
    def relation(cs):
        dl=lax.rem(cs-c+Z,Z)
        far=jnp.where(b==0,dl>=Z//2,(dl>=1)&(dl<=Z//2))
        do=lax.rem(cs-jnp.where(b==0,c-1,c+1)+2*Z,Z)
        out_near=jnp.where(b==0,(do>=1)&(do<=Z//2),do>=Z//2)
        return jnp.logical_not(far)|edge, out_near&jnp.logical_not(edge)
    def each(offs=NEAR):
        for off in offs:
            cs=lax.rem(c+off,Z)
            near,onear=relation(cs)
            for e in (0,1): yield near,onear,place(p,2*cs+e)
    def across(start):
        for near,onear,s in each():
            @pl.when(onear)
            def _():
                if start: landed(outer,s,router.at[s])
                k=remote(blk(outer,s),blk(own,s),sfwd.at[s],rown.at[s],side)
                k.start() if start else k.wait_send()
            @pl.when(near)
            def _():
                if start: landed(own,s,rown.at[s])
                k=remote(blk(own,s),blk(inner,s),sin.at[s],rinner.at[s],other)
                k.start() if start else k.wait_send()
            @pl.when(near&jnp.logical_not(edge))
            def _():
                k=remote(blk(own,s),blk(outer,s),sfwd.at[n+s],router.at[s],side)
                k.start() if start else k.wait_send()
            @pl.when(edge&open_)
            def _():
                k=remote(blk(own,s),blk(outer,s),sfwd.at[n+s],router.at[s],m,next_patch)
                k.start() if start else k.wait_send()
    def inside(start):
        for near,onear,s in each():
            @pl.when(jnp.logical_not(near))
            def _():
                if start: landed(own,s,rown.at[s])
                k=remote(blk(own,s),blk(inner,s),sin.at[s],rinner.at[s],other)
                k.start() if start else k.wait_send()
    across(True)
    inside(True)
    for near,onear,s in each():
        @pl.when(jnp.logical_not(onear)&open_)
        def _(): landed(outer,s,router.at[s])
        landed(inner,s,rinner.at[s])
    pltpu.make_async_copy(obs_out,obs_out,robs).wait()
    sends(sent,False)
    sends(sent,True)
    across(False)
    inside(False)


def front(x,fl,em,cells,count,values,scales):
    Bn,R,W=x.shape; V=pl.BlockSpec(memory_space=pltpu.VMEM); A=pl.BlockSpec(memory_space=pltpu.HBM); D=pltpu.SemaphoreType.DMA
    H=2*Bn+8; SL=cells.shape[1]; S=lambda *shape: pltpu.VMEM(shape,F32); n=R
    o=jax.ShapeDtypeStruct((R*Bn,W),F32)
    return pl.pallas_call(front_kernel,out_shape=(o,o,o,jax.ShapeDtypeStruct((8,SL),F32)),
        in_specs=[pl.BlockSpec(memory_space=pltpu.SMEM)]+[A]*6,out_specs=(V,)*4,
        scratch_shapes=[S(R,Bn,W),S(8,SL),S(Bn*R,128),S(Bn*R,128),S(4,R,W),S(1,Bn),pltpu.VMEM((1,SL),jnp.int32),S(1,SL),S(1,SL),S(R+4,Bn,W),S(R+2,Bn,W),S(4,R+8,W),S(2,H,W),S(2,H,W),
                        D((2,)),D((2,)),D((7,)),D((n,)),D((2*n,)),D((n,)),D((n,)),D((n,)),D((n,)),D,D],
        compiler_params=pltpu.CompilerParams(collective_id=0,has_side_effects=True,vmem_limit_bytes=20<<20),name='front')(count,*(pltpu.with_memory_space_constraint(a,pltpu.HBM) for a in (x.reshape(Bn*R,W),fl,em.reshape(1,Bn),cells,values,scales)))

def scatter_kernel(x_ref, out_ref, ssem, rsem, lsem):
    p=lax.axis_index('patch'); m=lax.axis_index('member'); n=out_ref.shape[0]; B=out_ref.shape[1]; row=place(p,m)
    barrier=pltpu.get_barrier_semaphore()
    for d in range(1,n):
        pl.semaphore_signal(barrier,inc=1,device_id=(p,lax.rem(m+d,n)),device_id_type=MESH)
    own=pltpu.make_async_copy(x_ref.at[pl.ds(pl.multiple_of(m*B,B),B)],out_ref.at[row],lsem)
    own.start()
    pl.semaphore_wait(barrier,n-1)
    cps=[]
    for d in [8,7,9,6,10,5,11,4,12,3,13,2,14,1,15]:
        to=lax.rem(m+d,n)
        c=pltpu.make_async_remote_copy(src_ref=x_ref.at[pl.ds(pl.multiple_of(to*B,B),B)],dst_ref=out_ref.at[row],
            send_sem=ssem.at[d],recv_sem=rsem.at[d],device_id=(p,to),device_id_type=MESH)
        c.start(); cps.append(c)
    own.wait()
    for c in cps: c.wait()
def scatter(x,n=16):
    A=pl.BlockSpec(memory_space=pltpu.VMEM)
    return pl.pallas_call(scatter_kernel,out_shape=jax.ShapeDtypeStruct((n,x.shape[0]//n,x.shape[1]),F32),
      in_specs=[A],out_specs=A,scratch_shapes=[pltpu.SemaphoreType.DMA((n,)),pltpu.SemaphoreType.DMA((n,)),pltpu.SemaphoreType.DMA],
      compiler_params=pltpu.CompilerParams(collective_id=1,has_side_effects=True,vmem_limit_bytes=16<<20),name='scatter')(x)


def per_device(
    init_field, flow_fields, emission, observed_cell, observed_count, observed_value, observed_scale
):
    gathered = front(
        init_field, flow_fields, emission, observed_cell, observed_count, observed_value, observed_scale
    )
    analysed = solve(*gathered)
    return jnp.transpose(scatter(analysed), (1, 0, 2))


def solution(mesh):
    return jax.shard_map(
        per_device,
        mesh=mesh,
        in_specs=(
            P("member", "patch", None),
            P(None, "patch", None),
            P("member"),
            P(("patch", "member"), None),
            P(("patch", "member")),
            P(("patch", "member"), None),
            P(("patch", "member"), None),
        ),
        out_specs=P("member", "patch", None),
        check_vma=False,
    )
```

```python
import functools
import math

import jax
import jax.numpy as jnp
from jax import lax
from jax.experimental import pallas as pl
from jax.experimental.pallas import tpu as pltpu
from jax.sharding import PartitionSpec as P

F32=jnp.float32; BF=jnp.bfloat16
HIGH=lax.Precision.HIGHEST
NT=(((1,),(1,)),((),())); TN=(((0,),(0,)),((),())); NN=(((1,),(0,)),((),()))
def bdot(a,b,dims): return lax.dot_general(a,b,dims,preferred_element_type=F32)
def split2(x):
    hi=x.astype(BF); lo=(x-hi.astype(F32)).astype(BF)
    return hi,lo

def tree(terms):
    while len(terms)>1:
        terms=[terms[a]+terms[a+1] if a+1<len(terms) else terms[a] for a in range(0,len(terms),2)]
    return terms[0]

def leaf_inverse(rows):
    G=len(rows); full=(8,128)
    lane=lax.broadcasted_iota(jnp.int32,full,1)
    sub=lax.broadcasted_iota(jnp.int32,full,0)
    down=lambda x,i: jnp.broadcast_to(x[i:i+1,:],full)
    for t in range(G):
        across=lambda g,j: jnp.broadcast_to(rows[g][:,8*t+j:8*t+j+1],full)
        inside=(lane>=8*t)&(lane<8*t+8)
        c=[across(t,j) for j in range(8)]
        src=[jnp.where(inside,jnp.where(lane==8*t+i,1.0,0.0),down(rows[t],i)) for i in range(8)]
        for p in range(8):
            r=1.0/down(c[p],p)
            at=sub==p
            mult=c[p]
            for j in range(8):
                if j==p: continue
                x=down(c[j],p)*r
                c[j]=jnp.where(at,x,c[j]-mult*x)
            c[p]=jnp.where(at,r,-(mult*r))
        new=tree([c[j]*src[j] for j in range(8)])
        rep=[down(new,i) for i in range(8)]
        out=[]
        for g in range(G):
            if g==t:
                out.append(new)
            else:
                out.append(jnp.where(inside,0.0,rows[g])-tree([across(g,i)*rep[i] for i in range(8)]))
        rows=out
    return rows

def solve_kernel(own_ref, outer_ref, inner_ref, obs_ref, ahi, alo, zh_ref, zl_ref, off_ref,
                 gt_ref, shi, slo, T):
    members=own_ref.shape[0]; W=own_ref.shape[1]; C=3*W; SL=obs_ref.shape[1]
    root=math.sqrt(members-1)
    patch=lax.axis_index('patch'); line=place(patch,lax.axis_index('member'))
    even=lax.rem(line,2)==0; closed=((patch==0)&(line==0))|((patch==lax.axis_size('patch')-1)&(line==15))
    j=lax.broadcasted_iota(jnp.int32,(1,SL),1)
    obs=obs_ref[...]
    act=jnp.where(j.astype(F32)<obs[1:2],1.0,0.0).astype(F32)
    w=act*obs[3:4]; w2=w*w; w2v=w2*obs[2:3]
    def split3(x):
        a=x.astype(BF).astype(F32); x=x-a; b=x.astype(BF).astype(F32); return a,b,x-b
    a0,a1,a2=split3(w2); b0,b1,b2=split3(w2v)
    lhs=jnp.concatenate([a0,a1,a2,b0,b1,b2,act,jnp.zeros_like(act)],axis=0).astype(BF)
    cell=obs[0:1].astype(jnp.int32)
    swapped=jnp.where(cell<W,cell+2*W,jnp.where(cell<2*W,cell,cell-2*W))
    cell=jnp.where(even,cell,swapped)
    et=(lax.broadcasted_iota(jnp.int32,(C,SL),0)==cell).astype(F32).astype(BF)
    sums=bdot(lhs,et,NT)
    lam=sums[0:1]+sums[1:2]+sums[2:3]
    bet=sums[3:4]+sums[4:5]+sums[5:6]
    present=sums[6:7]>0.5
    pres8=jnp.broadcast_to(jnp.where(present,1.0,0.0),(8,C)).astype(BF)
    tri=(lax.broadcasted_iota(jnp.int32,(C,C),0)<=lax.broadcasted_iota(jnp.int32,(C,C),1)).astype(F32).astype(BF)
    rank=bdot(pres8,tri,NN)[0:1]
    slot=jnp.where(present,rank-1.0,-1.0).astype(jnp.int32)
    gt_ref[...]=(lax.broadcasted_iota(jnp.int32,(SL,C),0)==slot).astype(F32).astype(BF)
    s=jnp.sqrt(lam)
    mus=[]
    for q,ref in enumerate((outer_ref,own_ref,inner_ref)):
        x=ref[...]
        if q==0: x=jnp.where(closed,0.0,x)
        mu=jnp.sum(x,axis=0,keepdims=True)*(1.0/members)
        mus.append(mu)
        sl=slice(q*W,(q+1)*W)
        h,l=split2((x-mu)*(s[:,sl]*(1.0/root)))
        ahi[:,sl]=h; alo[:,sl]=l
    mu=jnp.concatenate(mus,axis=1)
    d=jnp.where(present,(bet-lam*mu)/jnp.where(present,s,1.0),0.0)*(1.0/root)
    gt=gt_ref[...]
    shi[...]=bdot(gt,ahi[...],NT).astype(BF)
    slo[...]=bdot(gt,alo[...],NT).astype(BF)
    h,l=shi[...],slo[...]
    eye=(lax.broadcasted_iota(jnp.int32,(SL,SL),0)==lax.broadcasted_iota(jnp.int32,(SL,SL),1)).astype(F32)
    T[:,0:SL]=eye+bdot(h,h,NT)+(bdot(h,l,NT)+bdot(l,h,NT))
    oh,ol=split2(own_ref[...]-mus[1])
    T[:,SL:]=bdot(h,oh,NN)+(bdot(h,ol,NN)+bdot(l,oh,NN))
    total=jnp.max(rank)
    def step(k):
        o=k*128
        rows=leaf_inverse([T[o+8*g:o+8*g+8,o:o+128] for g in range(16)])
        dinv=jnp.concatenate(rows,axis=0)
        cuts=[(o+128,o+256),(o+256,SL+W)] if o+128<SL else [(SL,SL+W)]
        for lo,hi in cuts:
            U=jnp.dot(dinv,T[o:o+128,lo:hi],precision=HIGH,preferred_element_type=F32)
            T[o:o+128,lo:hi]=U
            order=[i for i in range(SL//128) if i!=k]
            order=[i for i in order if i>k]+[i for i in order if i<k]
            for i in order:
                T[i*128:i*128+128,lo:hi]=T[i*128:i*128+128,lo:hi]-jnp.dot(T[i*128:i*128+128,o:o+128],U,precision=HIGH,preferred_element_type=F32)
    for k in range(3): step(k)
    @pl.when(total>384.5)
    def _(): step(3)
    yh,yl=split2(T[:,SL:])
    zh=bdot(gt,yh,TN); zl=bdot(gt,yl,TN)
    off=jnp.dot(jnp.broadcast_to(d,(8,C)),zh+zl,precision=HIGH,preferred_element_type=F32)[0:1]
    zh_ref[...]=zh.astype(BF); zl_ref[...]=zl.astype(BF)
    off_ref[...]=jnp.broadcast_to(off,(8,W))

def solve(own,outer,inner,obs):
    m,W=own.shape; SL=obs.shape[1]; C=3*W
    V=pl.BlockSpec(memory_space=pltpu.VMEM)
    return pl.pallas_call(solve_kernel,out_shape=tuple(jax.ShapeDtypeStruct(*k) for k in (((m,C),BF),((m,C),BF),((C,W),BF),((C,W),BF),((8,W),F32))),in_specs=[V,V,V,V],out_specs=(V,)*5,
        scratch_shapes=[pltpu.VMEM((SL,C),BF),pltpu.VMEM((SL,m),BF),pltpu.VMEM((SL,m),BF),
                        pltpu.VMEM((SL,SL+W),F32)],
        compiler_params=pltpu.CompilerParams(vmem_limit_bytes=40<<20),name='solve')(own,outer,inner,obs)


MESH=pl.DeviceIdType.MESH

def place(p,l):
    return jnp.where(lax.rem(p,2)==0,l,15-l)

def front_kernel(count_ref, x_ref, fl_hbm, em_hbm, cell_hbm, value_hbm, scale_hbm, own, outer, inner, obs_out, fc, obs, xa, xb, fl_ref, em_ref, cell_ref, value_ref, scale_ref, fb, g1, flx, sbuf, rbuf, hsend, hrecv, lsem, ssend, sfwd, sin, rown, router, rinner, sobs, robs):
    n=16; Z=n//2
    P_=lax.axis_size('patch'); p=lax.axis_index('patch'); m=lax.axis_index('member')
    Bn=em_ref.shape[1]; R=x_ref.shape[0]//Bn; W=x_ref.shape[1]
    loads=[pltpu.make_async_copy(x_ref.at[:,h*128:(h+1)*128],t,lsem.at[h]) for h,t in enumerate((xa,xb))]
    small=[pltpu.make_async_copy(a,t,lsem.at[2+i]) for i,(a,t) in enumerate(((fl_hbm,fl_ref),(em_hbm,em_ref),(cell_hbm,cell_ref),(value_hbm,value_ref),(scale_hbm,scale_ref)))]
    for c in loads+small: c.start()
    barrier=pltpu.get_barrier_semaphore()
    up,dn=lax.rem(p+1,P_),lax.rem(p+P_-1,P_)
    for q in (up,dn): pl.semaphore_signal(barrier,inc=1,device_id=(q,m),device_id_type=MESH)
    for d in range(1,n):
        pl.semaphore_signal(barrier,inc=1,device_id=(p,lax.rem(m+d,n)),device_id_type=MESH)
    row=lambda r: jnp.concatenate([t[pl.ds(r,Bn,stride=R),:] for t in (xa,xb)],axis=1)
    for c in loads+small[:2]: c.wait()
    for i in range(2):
        sbuf[0,i*Bn:(i+1)*Bn]=row(i)
        sbuf[1,i*Bn:(i+1)*Bn]=row(R-2+i)
    for f in range(4):
        sbuf[0,2*Bn+2*f:2*Bn+2*f+2]=fl_ref[f,0:2]
        sbuf[1,2*Bn+2*f:2*Bn+2*f+2]=fl_ref[f,R-2:R]
    pl.semaphore_wait(barrier,n+1)
    cps=[]
    for k,q in ((0,dn),(1,up)):
        c=pltpu.make_async_remote_copy(src_ref=sbuf.at[k],dst_ref=rbuf.at[k],send_sem=hsend.at[k],recv_sem=hrecv.at[k],device_id=(q,m),device_id_type=MESH)
        c.start(); cps.append(c)
    eye=lax.broadcasted_iota(jnp.int32,(Bn,Bn),0)==lax.broadcasted_iota(jnp.int32,(Bn,Bn),1)
    em=jnp.sum(jnp.where(eye,jnp.broadcast_to(em_ref[...],(Bn,Bn)),0.0),axis=1,keepdims=True)
    emb=jnp.broadcast_to(em,(Bn,W))
    for f in range(4): flx[f,2:2+R]=fl_ref[f]
    for r in range(R): fb[r+2]=row(r)
    mlo=jnp.where(p>0,1.0,0.0); mhi=jnp.where(p<P_-1,1.0,0.0)
    def step(f,b,a,i):
        rf=flx[0,pl.ds(i,1),:]; cf=flx[1,pl.ds(i,1),:]; dc=flx[2,pl.ds(i,1),:]; so=flx[3,pl.ds(i,1),:]
        bc=pltpu.roll(f,1,1); ac=pltpu.roll(f,W-1,1)
        adv=(f-jnp.maximum(rf,0.0)*(f-b)-jnp.minimum(rf,0.0)*(a-f)-jnp.maximum(cf,0.0)*(f-bc)-jnp.minimum(cf,0.0)*(ac-f))
        return (1.0-dc)*adv+emb*so
    def once(r,mask=None):
        v=step(fb[r+2],fb[r+1],fb[r+3],r+2)
        g1[r+1]=v if mask is None else v*mask
    def second(r):
        fc[r]=step(g1[r+1],g1[r],g1[r+2],r+2)
    for c in small[2:]: c.wait()
    SL=obs.shape[1]
    for i in (0,4):
        obs[i:i+1]=cell_ref[...].astype(F32)
        obs[i+1:i+2]=jnp.broadcast_to(count_ref[0].astype(F32),(1,SL))
        obs[i+2:i+3]=value_ref[...]
        obs[i+3:i+4]=scale_ref[...]
    lax.fori_loop(1,R-1,lambda r,_:(once(r),0)[1],0)
    lax.fori_loop(2,R-2,lambda r,_:(second(r),0)[1],0)
    B=Bn
    l=place(p,m); c=l//2; b=lax.rem(l,2)
    first=(b==0)&(c==0); last=(b==1)&(c==Z-1); edge=first|last
    open_=jnp.logical_not((first&(p==0))|(last&(p==P_-1)))
    next_patch=jnp.where(first,p-1,p+1)
    blk=lambda ref,s: ref.at[pl.ds(pl.multiple_of(s*B,B),B)]
    def remote(src,dst,ss,rs,to,tp=None):
        return pltpu.make_async_remote_copy(src_ref=src,dst_ref=dst,send_sem=ss,recv_sem=rs,device_id=(p if tp is None else tp,to),device_id_type=MESH)
    def push(src,dst,ss,rs,to):
        @pl.when(to==m)
        def _(): pltpu.make_async_copy(src,dst,rs).start()
        @pl.when(to!=m)
        def _(): remote(src,dst,ss,rs,to).start()
    def sent(src,dst,ss,rs,to):
        @pl.when(to!=m)
        def _(): remote(src,dst,ss,rs,to).wait_send()
    def landed(ref,s,rs):
        d=blk(ref,s); pltpu.make_async_copy(d,d,rs).wait()
    def even_row(cr):
        dl=lax.rem(c-cr+Z,Z); left=(dl>=Z//2)&(cr>0)
        return left, place(p,jnp.where(left,2*cr-1,2*cr))
    def odd_row(cr):
        dl=lax.rem(c-cr+Z,Z); right=(dl>=1)&(dl<=Z//2)&(cr<Z-1)
        return right, place(p,jnp.where(right,2*cr+2,2*cr+1))
    NEAR=[0,1,7,2,6,3,5,4]
    def sends(act,ends):
        for off in NEAR:
            cr=lax.rem(c+off,Z); due=((cr==0)|(cr==Z-1)) if ends else ((cr>0)&(cr<Z-1))
            for odd in (0,1):
                via,to=(odd_row if odd else even_row)(cr)
                r=2*cr+odd
                src=fc.at[r]; ss=ssend.at[r]
                @pl.when(via&due)
                def _(): act(src,blk(outer,m),ss,router.at[m],to)
                @pl.when(jnp.logical_not(via)&due)
                def _(): act(src,blk(own,m),ss,rown.at[m],to)
        if not ends: act(obs,obs_out,sobs,robs,place(p,m))
    sends(push,False)
    for k_ in cps: k_.wait()
    for i in range(2):
        fb[i]=rbuf[1,i*Bn:(i+1)*Bn]*mlo
        fb[R+2+i]=rbuf[0,i*Bn:(i+1)*Bn]*mhi
    for f in range(4):
        flx[f,0:2]=rbuf[1,2*Bn+2*f:2*Bn+2*f+2]
        flx[f,R+2:R+4]=rbuf[0,2*Bn+2*f:2*Bn+2*f+2]
    for r,k in ((-1,mlo),(0,None),(R-1,None),(R,mhi)): once(r,k)
    for r in (0,1,R-2,R-1): second(r)

    sends(push,True)
    other=place(p,jnp.where(b==0,l+1,l-1))
    side=place(p,jnp.where(edge,l,jnp.where(b==0,l-1,l+1)))
    def relation(cs):
        dl=lax.rem(cs-c+Z,Z)
        far=jnp.where(b==0,dl>=Z//2,(dl>=1)&(dl<=Z//2))
        do=lax.rem(cs-jnp.where(b==0,c-1,c+1)+2*Z,Z)
        out_near=jnp.where(b==0,(do>=1)&(do<=Z//2),do>=Z//2)
        return jnp.logical_not(far)|edge, out_near&jnp.logical_not(edge)
    def each(offs=NEAR):
        for off in offs:
            cs=lax.rem(c+off,Z)
            near,onear=relation(cs)
            for e in (0,1): yield near,onear,place(p,2*cs+e)
    def across(start):
        for near,onear,s in each():
            @pl.when(onear)
            def _():
                if start: landed(outer,s,router.at[s])
                k=remote(blk(outer,s),blk(own,s),sfwd.at[s],rown.at[s],side)
                k.start() if start else k.wait_send()
            @pl.when(near)
            def _():
                if start: landed(own,s,rown.at[s])
                k=remote(blk(own,s),blk(inner,s),sin.at[s],rinner.at[s],other)
                k.start() if start else k.wait_send()
            @pl.when(near&jnp.logical_not(edge))
            def _():
                k=remote(blk(own,s),blk(outer,s),sfwd.at[n+s],router.at[s],side)
                k.start() if start else k.wait_send()
            @pl.when(edge&open_)
            def _():
                k=remote(blk(own,s),blk(outer,s),sfwd.at[n+s],router.at[s],m,next_patch)
                k.start() if start else k.wait_send()
    def inside(start):
        for near,onear,s in each():
            @pl.when(jnp.logical_not(near))
            def _():
                if start: landed(own,s,rown.at[s])
                k=remote(blk(own,s),blk(inner,s),sin.at[s],rinner.at[s],other)
                k.start() if start else k.wait_send()
    across(True)
    inside(True)
    for near,onear,s in each():
        @pl.when(jnp.logical_not(onear)&open_)
        def _(): landed(outer,s,router.at[s])
        landed(inner,s,rinner.at[s])
    pltpu.make_async_copy(obs_out,obs_out,robs).wait()
    sends(sent,False)
    sends(sent,True)
    across(False)
    inside(False)


def front(x,fl,em,cells,count,values,scales):
    Bn,R,W=x.shape; V=pl.BlockSpec(memory_space=pltpu.VMEM); A=pl.BlockSpec(memory_space=pltpu.HBM); D=pltpu.SemaphoreType.DMA
    H=2*Bn+8; SL=cells.shape[1]; S=lambda *shape: pltpu.VMEM(shape,F32); n=R
    o=jax.ShapeDtypeStruct((R*Bn,W),F32)
    return pl.pallas_call(front_kernel,out_shape=(o,o,o,jax.ShapeDtypeStruct((8,SL),F32)),
        in_specs=[pl.BlockSpec(memory_space=pltpu.SMEM)]+[A]*6,out_specs=(V,)*4,
        scratch_shapes=[S(R,Bn,W),S(8,SL),S(Bn*R,128),S(Bn*R,128),S(4,R,W),S(1,Bn),pltpu.VMEM((1,SL),jnp.int32),S(1,SL),S(1,SL),S(R+4,Bn,W),S(R+2,Bn,W),S(4,R+8,W),S(2,H,W),S(2,H,W),
                        D((2,)),D((2,)),D((7,)),D((n,)),D((2*n,)),D((n,)),D((n,)),D((n,)),D((n,)),D,D],
        compiler_params=pltpu.CompilerParams(collective_id=0,has_side_effects=True,vmem_limit_bytes=20<<20),name='front')(count,*(pltpu.with_memory_space_constraint(a,pltpu.HBM) for a in (x.reshape(Bn*R,W),fl,em.reshape(1,Bn),cells,values,scales)))

def scatter_kernel(own_ref, ahi, alo, zh, zl, off_ref, out_ref, block, ssem, rsem):
    p=lax.axis_index('patch'); m=lax.axis_index('member'); n=out_ref.shape[0]; B=out_ref.shape[1]; row=place(p,m)
    barrier=pltpu.get_barrier_semaphore()
    for d in range(1,n):
        pl.semaphore_signal(barrier,inc=1,device_id=(p,lax.rem(m+d,n)),device_id_type=MESH)
    def analysed(k):
        at=pl.ds(pl.multiple_of(k*B,B),B)
        h=ahi[at]
        sy=bdot(h,zh[...],NN)+(bdot(h,zl[...],NN)+bdot(alo[at],zh[...],NN))
        return own_ref[at]-0.5*sy+off_ref[0:1]
    cps=[]
    for i,d in enumerate([8,7,9,6,10,5,11,4,12,3,13,2,14,1,15]):
        to=lax.rem(m+d,n)
        block[d]=analysed(to)
        if i==0: pl.semaphore_wait(barrier,n-1)
        c=pltpu.make_async_remote_copy(src_ref=block.at[d],dst_ref=out_ref.at[row],
            send_sem=ssem.at[d],recv_sem=rsem.at[d],device_id=(p,to),device_id_type=MESH)
        c.start(); cps.append(c)
    out_ref[row]=analysed(m)
    for c in cps: c.wait()

def scatter(own,ahi,alo,zh,zl,off,n=16):
    A=pl.BlockSpec(memory_space=pltpu.VMEM); B=own.shape[0]//n; W=own.shape[1]; D=pltpu.SemaphoreType.DMA
    return pl.pallas_call(scatter_kernel,out_shape=jax.ShapeDtypeStruct((n,B,W),F32),
      in_specs=[A]*6,out_specs=A,scratch_shapes=[pltpu.VMEM((n,B,W),F32),D((n,)),D((n,))],
      compiler_params=pltpu.CompilerParams(collective_id=1,has_side_effects=True,vmem_limit_bytes=16<<20),name='scatter')(own,ahi,alo,zh,zl,off)


def per_device(
    init_field, flow_fields, emission, observed_cell, observed_count, observed_value, observed_scale
):
    gathered = front(
        init_field, flow_fields, emission, observed_cell, observed_count, observed_value, observed_scale
    )
    solved = solve(*gathered)
    return jnp.transpose(scatter(gathered[0], *solved), (1, 0, 2))


def solution(mesh):
    return jax.shard_map(
        per_device,
        mesh=mesh,
        in_specs=(
            P("member", "patch", None),
            P(None, "patch", None),
            P("member"),
            P(("patch", "member"), None),
            P(("patch", "member")),
            P(("patch", "member"), None),
            P(("patch", "member"), None),
        ),
        out_specs=P("member", "patch", None),
        check_vma=False,
    )
```
